512 devices in a mesh: cells: 128 (over y, z, core), genes: 4 (over x).
Axes of the slice: x: 4, y: 8, z: 8, core: 2. Of those that a mesh axis runs over, the one named last changes fastest.
Arguments:
- data: bfloat16 [131072, 2000], P('cells', 'genes'), may hold values from -6 to 6
- start: float32 [2000, 64], P('genes'), may hold values from -6 to 6
- link_dev: int32 [512, 8], P('cells'), may hold values from 0 to 127, all different within a row; in each aligned block of 4 rows (0 to 3, 4 to 7, ...) at most 2 rows name the same one
- link_slot: int32 [512, 8], P('cells'), may hold values from 0 to 3
- link_weight: int32 [512, 8], P('cells'), may hold values from 1 to 8
Outputs:
- loadings: float32 [2000, 64], P('genes')
- smoothed: bfloat16 [64, 131072], P('genes', 'cells')
The draws below stay inside these ranges and needn't reach their ends.
Inputs may be any that keep to these rules, and one draw needn't show every extreme that they name: `link_dev`: each row names 8 different devices; the tiles of one device name any one device in at most 2 links, and some device in exactly 2.
All inputs are finite; a program needn't handle non-finite values.
Results may differ from the reference program's by a relative error of at most 0.017.
Values may be sent and summed in bfloat16 or wider, within the bound.
A program may use at most 64 MiB of HBM per device.

```python
import math
import jax
import jax.numpy as jnp
import numpy as np
from jax import lax

G = 2000
K = 64
NB = 8
TILES_DEV = 4
ITERS = 3
NT = 512
CELLS = 131072
CAP = 2
N_CELLS = 128


def touch_ends(result, own_key, smallest, largest):
    extent = result.shape
    place = [jax.random.randint(jax.random.fold_in(own_key, axis), (), 0, extent[axis]) for axis in range(len(extent))]
    result = result.at[tuple(place)].set(smallest)
    longest = extent.index(max(extent))
    place[longest] = (place[longest] + 1) % extent[longest]
    return result.at[tuple(place)].set(largest)


def block_scale(rng, shape, split, least, high):
    level, own = 1.0, jax.random.fold_in(rng, 6)
    for axis_at, shards_of in split:
        heights = jnp.exp(jax.random.uniform(jax.random.fold_in(own, axis_at), (shards_of,), jnp.float32, least / len(split), high / len(split)))
        level = level * jnp.repeat(heights, shape[axis_at] // shards_of).reshape([-1 if axis == axis_at else 1 for axis in range(len(shape))])
    return level


def routed_block(stream_key, own, number, rows, amount, top, limit, skew):
    order = jax.random.permutation(stream_key, amount)
    packed, common = load_shares(amount, rows * top, limit, skew, True), load_shares(amount, rows * top, limit, skew, False)
    places = jnp.arange(amount)

    def named(sizes, turn):
        used = int((sizes > 0).sum())
        fixed = max(1, used // 4)
        moved = fixed + (places - fixed + turn * (used - fixed)) % max(1, amount - fixed)
        return jnp.zeros((amount,), jnp.int32).at[order[jnp.where(places < fixed, places, moved)]].set(jnp.asarray(sizes, jnp.int32))

    sizes = jnp.where(number % 4 == 0, named(packed, number // 4), named(common, number - number // 4 - 1))
    mixed = jax.random.permutation(jax.random.fold_in(own, 3), amount)
    donor, sink = mixed[0:amount // 2 * 2:2], mixed[1:amount // 2 * 2:2]
    slack = jnp.minimum(sizes[donor] - 1, limit - sizes[sink]) // 2
    slack = jnp.where((donor == order[0]) | (sink == order[0]) | (sizes[sink] == 0), 0, jnp.maximum(slack, 0))
    moved = jax.random.randint(jax.random.fold_in(own, 4), (amount // 2,), 0, 1 << 20) % (slack + 1)
    sizes = sizes.at[donor].add(-moved).at[sink].add(moved)
    labels = jnp.searchsorted(jnp.cumsum(sizes), jnp.arange(rows * top), side="right").astype(jnp.int32)
    listing = labels.reshape(top, rows).T
    listing = listing[jax.random.permutation(jax.random.fold_in(own, 1), rows)]
    turn = jax.random.randint(jax.random.fold_in(own, 2), (rows, 1), 0, top)
    return jnp.take_along_axis(listing, (jnp.arange(top)[None, :] + turn) % top, axis=1)


def load_shares(number_of, total, reach, lean, full):
    weights = [(1 << 20) // math.isqrt(rank ** lean) + 1 for rank in range(1, number_of + 1)]
    largest = reach if full else min(reach, max(-(-total // number_of), total * weights[0] // sum(weights)))
    least = 1 if total - largest >= number_of - 1 else 0
    given, rest = [largest] + [least] * (number_of - 1), total - largest - least * (number_of - 1)
    while rest > 0:
        candidates = [i for i in range(1, number_of) if given[i] < largest] or [i for i in range(1, number_of) if given[i] < reach]
        pool, budget = sum([weights[i] for i in candidates]), rest
        for i in candidates:
            extra = min(reach - given[i], max(1, budget * weights[i] // pool), rest)
            given[i] = given[i] + extra
            rest = rest - extra
    return np.array(given)


def bell_draw(rng, shape, scale, most, cuts=(), held_as=jnp.bfloat16):
    drawn = scale * jax.random.normal(rng, shape, jnp.float32)
    if cuts:
        drawn = drawn * block_scale(rng, shape, cuts, -0.22, 0.18)
    return jnp.clip(drawn, -most, most).astype(held_as)


def setup_inputs(seed: int = 0) -> dict:
    splits = jax.random.split(jax.random.key(seed), 6)
    data = bell_draw(splits[0], (CELLS, G), 1.0, 6.0, ((0, 128), (1, 4)))
    start = bell_draw(splits[1], (G, K), 1.0, 6.0, ((0, 4),), jnp.float32)
    link_dev_keys = jax.random.split(jax.random.fold_in(splits[2], 1), NT // TILES_DEV)
    link_dev_turns = jax.random.permutation(jax.random.fold_in(splits[2], 3), NT // TILES_DEV)
    link_dev = jax.vmap(lambda own, number: routed_block(jax.random.fold_in(splits[2], 2), own, number, TILES_DEV, N_CELLS, NB, CAP, 2))(link_dev_keys, link_dev_turns).reshape((NT, NB))
    link_slot = touch_ends(jax.random.randint(splits[3], (NT, NB), 0, TILES_DEV), jax.random.fold_in(splits[3], 1), 0, TILES_DEV - 1).astype(jnp.int32)
    link_weight = touch_ends(jax.random.randint(splits[4], (NT, NB), 1, 9), jax.random.fold_in(splits[4], 1), 1, 8).astype(jnp.int32)
    return dict(data=data, start=start, link_dev=link_dev, link_slot=link_slot, link_weight=link_weight)


self_weight = 8.0

def reference(data, start, link_dev, link_slot, link_weight):
    tiles_total = link_dev.shape[0]
    tile_cells = data.shape[0] // tiles_total
    width = start.shape[1]
    genes_total = data.shape[1]
    target = (link_dev * TILES_DEV + link_slot).astype(jnp.int32)
    weight = link_weight.astype(jnp.float32)
    degree = self_weight + lax.optimization_barrier(jnp.sum(weight, axis=1))
    scale = degree[:, None, None]
    loadings = start
    second = jnp.zeros((data.shape[0], width), jnp.bfloat16)
    for step in range(ITERS):
        narrow = loadings.astype(jnp.bfloat16)
        scores = (jnp.dot(data.astype(jnp.float32), narrow.astype(jnp.float32), preferred_element_type=jnp.float32) / math.sqrt(genes_total)).astype(jnp.bfloat16)
        blocks = scores.reshape(tiles_total, tile_cells, width).astype(jnp.float32)
        total = self_weight * blocks
        for slot in range(NB):
            total = total + weight[:, slot][:, None, None] * blocks[target[:, slot]]
        first = lax.optimization_barrier((total / scale).astype(jnp.bfloat16)).astype(jnp.float32)
        spread = lax.optimization_barrier((self_weight * first / scale).astype(jnp.bfloat16)).astype(jnp.float32)
        pushed = self_weight * spread
        for slot in range(NB):
            pushed = pushed.at[target[:, slot]].add(weight[:, slot][:, None, None] * spread)
        second = pushed.astype(jnp.bfloat16).reshape(tiles_total * tile_cells, width)
        update = lax.dot_general(data.astype(jnp.float32), second.astype(jnp.float32), (((0,), (0,)), ((), ())), preferred_element_type=jnp.float32)
        gram = jnp.dot(update.T.astype(jnp.float32), update.astype(jnp.float32), precision=lax.Precision.HIGHEST, preferred_element_type=jnp.float32) / genes_total
        factor = jnp.linalg.cholesky(gram)
        loadings = lax.linalg.triangular_solve(factor, update, left_side=False, lower=True, transpose_a=True)
    return (loadings, second.T)
```

```python
import math

import jax
import jax.numpy as jnp
from jax import lax
from jax.experimental import pallas as pl
from jax.experimental.pallas import tpu as pltpu
from jax.sharding import PartitionSpec as P

ITERS = 3
MESH = pl.DeviceIdType.MESH
SELF = 8.0
RING = 16
F32, BF16 = jnp.float32, jnp.bfloat16
HIGH = lax.Precision.HIGHEST


def inverse_factor(gram):
    n = gram.shape[0]
    row_at = lax.broadcasted_iota(jnp.int32, (8, 2 * n), 0)
    lane_at = lax.broadcasted_iota(jnp.int32, (8, 2 * n), 1)
    blocks = []
    for b in range(n // 8):
        eye = (lane_at == row_at + (n + 8 * b)).astype(F32)
        blocks.append(jnp.where(lane_at < n, gram[8 * b : 8 * b + 8], eye))
    scales = []
    for k in range(n):
        at, sub = divmod(k, 8)
        row = blocks[at][sub : sub + 1, :]
        pivot = row[:, k : k + 1]
        scaled = row * (1.0 / pivot)
        scales.append(lax.rsqrt(pivot))
        for b in range(at, n // 8):
            column = blocks[b][:, k : k + 1]
            change = column * scaled
            if b == at:
                change = jnp.where(row_at > sub, change, 0.0)
            blocks[b] = blocks[b] - change
    out = []
    for b in range(n // 8):
        scale = jnp.zeros((8, 1), F32)
        for sub in range(8):
            scale = jnp.where(row_at[:, :1] == sub, scales[8 * b + sub], scale)
        out.append(blocks[b][:, n:] * scale)
    return jnp.concatenate(out, axis=0)


def power_kernel(
    genes_total, groups, rings,
    y_ref, yt_ref, start_ref,
    q_out, z_out,
    z_send, z_got, s_got, u_send, u_got, v_got, w_got, g_got, full, q_ref,
    z_ss, z_rs, s_ss, s_rs, u_ss, u_rs, v_ss, v_rs, w_ss, w_rs, g_ss, g_rs,
):
    cell, group = lax.axis_index("cells"), lax.axis_index("genes")
    ring, spot = cell // RING, lax.rem(cell, RING)
    x_peers = [((cell, lax.rem(group + d, groups)), lax.rem(group + d, groups)) for d in range(1, groups)]
    z_peers = [
        ((ring * RING + lax.rem(spot + d, RING), group), lax.rem(spot + d, RING)) for d in range(1, RING)
    ]
    y_peers = [
        ((lax.rem(ring + d, rings) * RING + spot, group), lax.rem(ring + d, rings)) for d in range(1, rings)
    ]
    barrier = pltpu.get_barrier_semaphore()
    for device, _ in x_peers + z_peers + y_peers:
        pl.semaphore_signal(barrier, inc=1, device_id=device, device_id_type=MESH)
    pl.semaphore_wait(barrier, len(x_peers) + len(z_peers) + len(y_peers))

    def exchange(peers, me, source, got, send, receive):
        copies = [
            pltpu.make_async_remote_copy(
                src_ref=source(at), dst_ref=got.at[me], send_sem=send.at[at], recv_sem=receive.at[me],
                device_id=device, device_id_type=MESH,
            )
            for device, at in peers
        ]
        for copy in copies:
            copy.start()

        def finish():
            for device, at in peers:
                pltpu.make_async_remote_copy(
                    src_ref=source(at), dst_ref=got.at[at], send_sem=send.at[at], recv_sem=receive.at[at],
                    device_id=device, device_id_type=MESH,
                ).wait_recv()
            for copy in copies:
                copy.wait_send()

        return finish

    width, genes = start_ref.shape
    part = width // groups
    half = genes // 2
    q_ref[...] = start_ref[...].astype(BF16)
    for step in range(ITERS):
        partial = jnp.dot(q_ref[...], yt_ref[...], preferred_element_type=F32).astype(BF16)
        for g in range(groups):
            z_send[step, g] = partial[part * g : part * (g + 1)]
        finish = exchange(x_peers, group, lambda at: z_send.at[step, at], z_got.at[step], z_ss.at[step], z_rs.at[step])
        z_got[step, group] = z_send[step, group]
        finish()
        mine = z_got[step, 0].astype(F32)
        for g in range(1, groups):
            mine = mine + z_got[step, g].astype(F32)
        mine = mine.astype(BF16)
        if step == ITERS - 1:
            z_out[...] = mine
        s_got[step, group] = mine
        finish = exchange(x_peers, group, lambda at: s_got.at[step, group], s_got.at[step], s_ss.at[step], s_rs.at[step])
        finish()
        scores = jnp.concatenate([s_got[step, g] for g in range(groups)], axis=0)
        update = jnp.dot(scores, y_ref[...], preferred_element_type=F32)
        for s in range(RING):
            a, b = divmod(s, 2)
            u_send[step, s] = update[8 * a : 8 * a + 8, half * b : half * (b + 1)]
        finish = exchange(z_peers, spot, lambda at: u_send.at[step, at], u_got.at[step], u_ss.at[step], u_rs.at[step])
        u_got[step, spot] = u_send[step, spot]
        finish()
        total = u_got[step, 0]
        for s in range(1, RING):
            total = total + u_got[step, s]
        v_got[step, ring] = total
        finish = exchange(y_peers, ring, lambda at: v_got.at[step, ring], v_got.at[step], v_ss.at[step], v_rs.at[step])
        finish()
        total = v_got[step, 0]
        for s in range(1, rings):
            total = total + v_got[step, s]
        w_got[step, spot] = total
        finish = exchange(z_peers, spot, lambda at: w_got.at[step, spot], w_got.at[step], w_ss.at[step], w_rs.at[step])
        finish()
        for s in range(RING):
            a, b = divmod(s, 2)
            full[8 * a : 8 * a + 8, half * b : half * (b + 1)] = w_got[step, s]
        update = full[...]
        g_got[step, group] = lax.dot_general(
            update, update, (((1,), (1,)), ((), ())), precision=HIGH, preferred_element_type=F32
        )
        finish = exchange(x_peers, group, lambda at: g_got.at[step, group], g_got.at[step], g_ss.at[step], g_rs.at[step])
        finish()
        gram = g_got[step, 0]
        for g in range(1, groups):
            gram = gram + g_got[step, g]
        gram = gram * (1.0 / genes_total)
        gram = jnp.concatenate([gram, jnp.zeros_like(gram)], axis=1)
        factor = inverse_factor(gram)
        loadings = jnp.dot(factor, full[...], precision=HIGH, preferred_element_type=F32)
        if step == ITERS - 1:
            q_out[...] = loadings
        else:
            q_ref[...] = loadings.astype(BF16)


def per_device(data, start, link_dev, link_slot, link_weight):
    devices = lax.axis_size("cells")
    groups = lax.axis_size("genes")
    tiles_here, neighbours = link_dev.shape
    cells_here, genes_here = data.shape
    tile_cells = cells_here // tiles_here
    turns = tile_cells // devices
    genes_total = genes_here * groups
    width = start.shape[1]
    part = width // groups
    tiles_all = tiles_here * devices
    rings = devices // RING
    lanes = -(-genes_here // 128) * 128
    spare = lanes - genes_here
    table = jnp.concatenate([link_dev, link_slot, link_weight], axis=1).astype(BF16)
    table = table.reshape(tiles_here, turns, 1, spare)
    packed = jnp.concatenate(
        [
            data.reshape(tiles_here, turns, devices, genes_here),
            jnp.broadcast_to(table, (tiles_here, turns, devices, spare)),
        ],
        axis=3,
    )
    packed = packed.transpose(2, 0, 1, 3).reshape(devices, tiles_here * turns, lanes)
    moved = lax.all_to_all(packed, "cells", split_axis=0, concat_axis=0, tiled=True)
    moved = moved.reshape(tiles_all, turns, lanes).transpose(1, 0, 2)
    tables = moved[:, :, genes_here:].transpose(1, 0, 2).reshape(tiles_all, 3 * neighbours)
    tables = tables.astype(jnp.int32)
    target = tables[:, :neighbours] * tiles_here + tables[:, neighbours : 2 * neighbours]
    weight = tables[:, 2 * neighbours :].astype(F32)
    degree = SELF + jnp.sum(weight, axis=1)
    scale = (math.sqrt(SELF / math.sqrt(genes_total)) / degree)[:, None]
    tile_ids = jnp.arange(tiles_all, dtype=jnp.int32)
    links = SELF * (tile_ids[:, None] == tile_ids[None, :]).astype(F32)
    for j in range(neighbours):
        links = links + jnp.where(target[:, j : j + 1] == tile_ids[None, :], weight[:, j : j + 1], 0.0)
    links = links.astype(BF16)
    clean = jnp.where(jnp.arange(lanes) < genes_here, moved, jnp.zeros((), BF16))
    spreading = [jnp.dot(links, clean[i], preferred_element_type=F32) * scale for i in range(turns)]
    y = jnp.concatenate(spreading, axis=0).astype(BF16)
    yt = y.T
    qt = jnp.pad(start.T, ((0, 0), (0, spare)))

    vmem = pl.BlockSpec(memory_space=pltpu.VMEM)
    half = lanes // 2
    dma = pltpu.SemaphoreType.DMA
    sems = []
    for count in (groups, groups, RING, rings, RING, groups):
        sems += [dma((ITERS, count)), dma((ITERS, count))]
    loadings, last = pl.pallas_call(
        lambda *refs: power_kernel(genes_total, groups, rings, *refs),
        out_shape=(
            jax.ShapeDtypeStruct((width, lanes), F32),
            jax.ShapeDtypeStruct((part, turns * tiles_all), BF16),
        ),
        in_specs=[vmem] * 3,
        out_specs=(vmem, vmem),
        scratch_shapes=[
            pltpu.VMEM((ITERS, groups, part, turns * tiles_all), BF16),
            pltpu.VMEM((ITERS, groups, part, turns * tiles_all), BF16),
            pltpu.VMEM((ITERS, groups, part, turns * tiles_all), BF16),
            pltpu.VMEM((ITERS, RING, 8, half), F32),
            pltpu.VMEM((ITERS, RING, 8, half), F32),
            pltpu.VMEM((ITERS, rings, 8, half), F32),
            pltpu.VMEM((ITERS, RING, 8, half), F32),
            pltpu.VMEM((ITERS, groups, width, width), F32),
            pltpu.VMEM((width, lanes), F32),
            pltpu.VMEM((width, lanes), BF16),
            *sems,
        ],
        compiler_params=pltpu.CompilerParams(collective_id=0, has_side_effects=True),
        name="power",
    )(y, yt, qt)

    sent = (last.reshape(part, turns, tiles_all).astype(F32) * scale[:, 0]).astype(BF16)
    second = jnp.dot(sent.reshape(part * turns, tiles_all), links, preferred_element_type=F32).astype(BF16)
    second = second.reshape(part, turns, devices, tiles_here).transpose(2, 0, 3, 1)
    second = second.reshape(devices, part * tiles_here * turns)
    second = lax.all_to_all(second, "cells", split_axis=0, concat_axis=0, tiled=True)
    smoothed = second.T.reshape(part, tiles_here * turns * devices)
    return loadings[:, :genes_here].T, smoothed


def solution(mesh):
    placed = (
        P("cells", "genes"),
        P("genes", None),
        P("cells", None),
        P("cells", None),
        P("cells", None),
    )
    return jax.shard_map(
        per_device,
        mesh=mesh,
        in_specs=placed,
        out_specs=(P("genes", None), P("genes", "cells")),
        check_vma=False,
    )
```

```python
import math

import jax
import jax.numpy as jnp
from jax import lax
from jax.experimental import pallas as pl
from jax.experimental.pallas import tpu as pltpu
from jax.sharding import PartitionSpec as P

ITERS = 3
MESH = pl.DeviceIdType.MESH
SELF = 8.0
RING = 16
TILES, TURNS = 4, 2
F32, BF16 = jnp.float32, jnp.bfloat16
HIGH = lax.Precision.HIGHEST


def inverse_factor(gram):
    n = gram.shape[0]
    row_at = lax.broadcasted_iota(jnp.int32, (8, 2 * n), 0)
    lane_at = lax.broadcasted_iota(jnp.int32, (8, 2 * n), 1)
    blocks = []
    for b in range(n // 8):
        eye = (lane_at == row_at + (n + 8 * b)).astype(F32)
        blocks.append(jnp.where(lane_at < n, gram[8 * b : 8 * b + 8], eye))
    scales = []
    for k in range(n):
        at, sub = divmod(k, 8)
        row = blocks[at][sub : sub + 1, :]
        pivot = row[:, k : k + 1]
        scaled = row * (1.0 / pivot)
        scales.append(lax.rsqrt(pivot))
        for b in range(at, n // 8):
            column = blocks[b][:, k : k + 1]
            change = column * scaled
            if b == at:
                change = jnp.where(row_at > sub, change, 0.0)
            blocks[b] = blocks[b] - change
    out = []
    for b in range(n // 8):
        scale = jnp.zeros((8, 1), F32)
        for sub in range(8):
            scale = jnp.where(row_at[:, :1] == sub, scales[8 * b + sub], scale)
        out.append(blocks[b][:, n:] * scale)
    return jnp.concatenate(out, axis=0)


def one_hot(outs, ins, place):
    row = lax.broadcasted_iota(jnp.int32, (outs, ins), 0)
    column = lax.broadcasted_iota(jnp.int32, (outs, ins), 1)
    return (column == place(row)).astype(F32).astype(BF16)


def pick(matrix, rows):
    return jnp.dot(matrix, rows, preferred_element_type=F32).astype(BF16)


NT = (((1,), (1,)), ((), ()))


def power_kernel(
    genes_total, genes_here, groups, rings,
    x_ref, start_ref,
    q_out, s_out,
    a1_got, a2_send, a2_got, b1_send, b1_got, b2_send, b2_got, d_ref, links_ref, tail_ref, y_ref, yt_ref,
    f1_send, f1_got, f2_send, f2_got,
    z_send, z_got, s_got, u_send, u_got, v_got, w_got, g_got, full, q_ref, start_pad,
    a1_ss, a1_rs, a2_ss, a2_rs, b1_ss, b1_rs, b2_ss, b2_rs, f1_ss, f1_rs, f2_ss, f2_rs,
    z_ss, z_rs, s_ss, s_rs, u_ss, u_rs, v_ss, v_rs, w_ss, w_rs, g_ss, g_rs,
):
    cell, group = lax.axis_index("cells"), lax.axis_index("genes")
    ring, spot = cell // RING, lax.rem(cell, RING)
    layer, core = spot // 2, lax.rem(spot, 2)
    depth = RING // 2
    far = lambda n: sorted(range(1, n), key=lambda d: (-min(d, n - d), d))
    x_peers = [((cell, lax.rem(group + d, groups)), lax.rem(group + d, groups)) for d in far(groups)]
    z_peers = []
    for d in far(depth) + [0]:
        for e in (0, 1):
            if d or e:
                at = lax.rem(layer + d, depth) * 2 + lax.rem(core + e, 2)
                z_peers.append(((ring * RING + at, group), at))
    y_peers = [
        ((lax.rem(ring + d, rings) * RING + spot, group), lax.rem(ring + d, rings)) for d in far(rings)
    ]
    barrier = pltpu.get_barrier_semaphore()
    for device, _ in x_peers + z_peers + y_peers:
        pl.semaphore_signal(barrier, inc=1, device_id=device, device_id_type=MESH)
    pl.semaphore_wait(barrier, len(x_peers) + len(z_peers) + len(y_peers))

    def exchange(peers, me, source, got, send, receive):
        copies = [
            pltpu.make_async_remote_copy(
                src_ref=source(at), dst_ref=got.at[me], send_sem=send.at[at], recv_sem=receive.at[me],
                device_id=device, device_id_type=MESH,
            )
            for device, at in peers
        ]
        for copy in copies:
            copy.start()

        def finish():
            for device, at in peers:
                pltpu.make_async_remote_copy(
                    src_ref=source(at), dst_ref=got.at[at], send_sem=send.at[at], recv_sem=receive.at[at],
                    device_id=device, device_id_type=MESH,
                ).wait_recv()
            for copy in copies:
                copy.wait_send()

        return finish

    tiles, genes = d_ref.shape[1], d_ref.shape[2]
    width = start_ref.shape[1]
    part = width // groups
    half = genes // 2
    pairs = depth // 2

    finish_a1 = exchange(z_peers, spot, lambda at: x_ref.at[:, at, :, pl.ds(0, half)], a1_got, a1_ss, a1_rs)
    order = one_hot(256, 256, lambda o: ((o >> 1) & 15) * 16 + (o >> 5) * 2 + (o & 1))
    for t in range(TILES):
        rows = pick(order, x_ref[t, :, :, half:].reshape(256, half))
        b1_send[:, t] = rows.reshape(rings, 32, half)
    finish_b1 = exchange(y_peers, ring, lambda at: b1_send.at[at], b1_got, b1_ss, b1_rs)
    a1_got[spot] = x_ref[:, spot, :, 0:half]
    b1_got[ring] = b1_send[ring]
    start_pad[genes - 16 :] = jnp.zeros((16, width), F32)
    start_pad[0:genes_here] = start_ref[...]
    q_ref[...] = start_pad[...].T.astype(BF16)
    order_a = one_hot(256, 256, lambda o: ((o >> 3) & 3) * 64 + ((o >> 1) & 3) * 16 + (o >> 5) * 2 + (o & 1))
    order_b = one_hot(256, 256, lambda o: ((o >> 3) & 1) * 128 + ((o >> 1) & 3) * 32 + (o >> 4) * 2 + (o & 1))
    last_a = one_hot(256, 256, lambda o: (o & 127) * 2 + (o >> 7))
    last_b = one_hot(
        256, 256, lambda o: ((o >> 2) & 3) * 64 + ((o >> 4) & 7) * 8 + (o & 3) * 2 + (o >> 7)
    )
    finish_a1()
    for j in range(pairs):
        rows = pick(order_a, a1_got[4 * j : 4 * j + 4].reshape(256, half))
        a2_send[:, j] = rows.reshape(rings, 32, half)
    finish_a2 = exchange(y_peers, ring, lambda at: a2_send.at[at], a2_got, a2_ss, a2_rs)
    a2_got[ring] = a2_send[ring]
    finish_b1()
    for j in range(pairs):
        rows = pick(order_b, b1_got[2 * j : 2 * j + 2].reshape(256, half))
        b2_send[:, j] = rows.reshape(RING, 16, half)
    finish_b2 = exchange(z_peers, spot, lambda at: b2_send.at[at], b2_got, b2_ss, b2_rs)
    b2_got[spot] = b2_send[spot]
    finish_a2()
    for j in range(pairs):
        rows = pick(last_a, a2_got[2 * j : 2 * j + 2].reshape(256, half))
        for i in range(TURNS):
            d_ref[i, 128 * j : 128 * (j + 1), 0:half] = rows[128 * i : 128 * (i + 1)]
    finish_b2()
    for j in range(pairs):
        rows = pick(last_b, b2_got[4 * j : 4 * j + 4].reshape(256, half))
        for i in range(TURNS):
            for r in range(rings):
                d_ref[i, 64 * r + 16 * j : 64 * r + 16 * (j + 1), half:] = rows[
                    128 * i + 16 * r : 128 * i + 16 * (r + 1)
                ]

    root = math.sqrt(SELF / math.sqrt(genes_total))
    lane = lax.broadcasted_iota(jnp.int32, (32, tiles), 1)
    row_at = lax.broadcasted_iota(jnp.int32, (32, tiles), 0)

    def build(i, carry):
        at = pl.multiple_of(i * 32, 32)
        one = d_ref[0, pl.ds(at, 32), genes - 128 :].astype(F32)
        two = d_ref[1, pl.ds(at, 32), genes - 128 :].astype(F32)
        links = jnp.where(lane == row_at + at, SELF, 0.0)
        whole = lane.astype(F32)
        for j in range(8):
            device = one[:, 116 + j : 117 + j]
            place = one[:, 124 + j : 125 + j] if j < 4 else two[:, 112 + j : 113 + j]
            links = links + jnp.where(whole == device * TILES + place, two[:, 120 + j : 121 + j], 0.0)
        links_ref[pl.ds(at, 32)] = links.astype(BF16)
        return carry

    lax.fori_loop(0, tiles // 32, build, 0)
    tail = d_ref[1, :, genes - 128 :].astype(F32)
    tail_lane = lax.broadcasted_iota(jnp.int32, tail.shape, 1)
    scale = root / (SELF + jnp.sum(jnp.where(tail_lane >= 120, tail, 0.0), axis=1, keepdims=True))
    gene_lane = lax.broadcasted_iota(jnp.int32, (tiles, genes), 1)
    for i in range(TURNS):
        rows = jnp.dot(links_ref[...], d_ref[i], preferred_element_type=F32) * scale
        rows = jnp.where(gene_lane < genes_here, rows, 0.0).astype(BF16)
        y_ref[tiles * i : tiles * (i + 1)] = rows
        yt_ref[:, tiles * i : tiles * (i + 1)] = rows.T

    for step in range(ITERS):
        final = step == ITERS - 1
        partial = jnp.dot(q_ref[...], yt_ref[...], preferred_element_type=F32).astype(BF16)
        for g in range(groups):
            z_send[step, g] = partial[part * g : part * (g + 1)]
        finish = exchange(x_peers, group, lambda at: z_send.at[step, at], z_got.at[step], z_ss.at[step], z_rs.at[step])
        z_got[step, group] = z_send[step, group]
        if final:
            total_links = lax.dot_general(jnp.ones((8, tiles), BF16), links_ref[...], NT, preferred_element_type=F32)
            tail_scale = root / total_links[0:1]
        finish()
        mine = z_got[step, 0].astype(F32)
        for g in range(1, groups):
            mine = mine + z_got[step, g].astype(F32)
        mine = mine.astype(BF16)
        s_got[step, group] = mine
        finish = exchange(x_peers, group, lambda at: s_got.at[step, group], s_got.at[step], s_ss.at[step], s_rs.at[step])
        if final:
            sent = [(mine[:, tiles * i : tiles * (i + 1)].astype(F32) * tail_scale).astype(BF16) for i in range(TURNS)]
            sent = jnp.concatenate(sent + [jnp.zeros((128 - TURNS * part, tiles), BF16)], axis=0)
            second = lax.dot_general(tail_ref[...], sent, NT, preferred_element_type=F32).astype(BF16)
            f1_send[...] = second.reshape(f1_send.shape)
            finish_f1 = exchange(z_peers, spot, lambda at: f1_send.at[at], f1_got, f1_ss, f1_rs)
            f1_got[spot] = f1_send[spot]
        finish()
        scores = jnp.concatenate([s_got[step, g] for g in range(groups)], axis=0)
        update = jnp.dot(scores, y_ref[...], preferred_element_type=F32)
        for s in range(RING):
            a, b = divmod(s, 2)
            u_send[step, s] = update[8 * a : 8 * a + 8, half * b : half * (b + 1)]
        finish = exchange(z_peers, spot, lambda at: u_send.at[step, at], u_got.at[step], u_ss.at[step], u_rs.at[step])
        u_got[step, spot] = u_send[step, spot]
        if step == 0:
            order = one_hot(tiles, tiles, lambda o: ((o >> 2) & 7) * 64 + (o >> 5) * 4 + (o & 3))
            tail_ref[...] = lax.dot_general(order, links_ref[...], NT, preferred_element_type=F32).astype(BF16)
        if final:
            finish_f1()
            order = one_hot(tiles, tiles, lambda o: ((o >> 2) & 15) * 32 + (o >> 6) * 4 + (o & 3))
            f2_send[...] = pick(order, f1_got[...].reshape(tiles, 128)).reshape(f2_send.shape)
            finish_f2 = exchange(y_peers, ring, lambda at: f2_send.at[at], f2_got, f2_ss, f2_rs)
            f2_got[ring] = f2_send[ring]
        finish()
        total = u_got[step, 0]
        for s in range(1, RING):
            total = total + u_got[step, s]
        v_got[step, ring] = total
        finish = exchange(y_peers, ring, lambda at: v_got.at[step, ring], v_got.at[step], v_ss.at[step], v_rs.at[step])
        finish()
        total = v_got[step, 0]
        for s in range(1, rings):
            total = total + v_got[step, s]
        w_got[step, spot] = total
        finish = exchange(z_peers, spot, lambda at: w_got.at[step, spot], w_got.at[step], w_ss.at[step], w_rs.at[step])
        if final:
            finish_f2()
            turned = f2_got[...].reshape(tiles, 128).astype(F32).T.astype(BF16)
            cells = s_out.shape[1]
            row = lax.broadcasted_iota(jnp.int32, (tiles, cells), 0)
            column = lax.broadcasted_iota(jnp.int32, (tiles, cells), 1)
            spread = column == (row & 3) * 256 + ((row >> 2) & 15) * 16 + (row >> 6) * 2
            spread = spread.astype(F32).astype(BF16)
            even = jnp.dot(turned[0:part], spread, preferred_element_type=F32)
            odd = jnp.dot(turned[part : 2 * part], spread, preferred_element_type=F32)
            s_out[...] = (even + pltpu.roll(odd, 1, 1)).astype(BF16)
        finish()
        for s in range(RING):
            a, b = divmod(s, 2)
            full[8 * a : 8 * a + 8, half * b : half * (b + 1)] = w_got[step, s]
        update = full[...]
        g_got[step, group] = lax.dot_general(update, update, NT, precision=HIGH, preferred_element_type=F32)
        finish = exchange(x_peers, group, lambda at: g_got.at[step, group], g_got.at[step], g_ss.at[step], g_rs.at[step])
        finish()
        gram = g_got[step, 0]
        for g in range(1, groups):
            gram = gram + g_got[step, g]
        gram = gram * (1.0 / genes_total)
        gram = jnp.concatenate([gram, jnp.zeros_like(gram)], axis=1)
        factor = inverse_factor(gram)
        loadings = jnp.dot(factor, full[...], precision=HIGH, preferred_element_type=F32)
        if final:
            q_out[...] = loadings.T[0:genes_here]
        else:
            q_ref[...] = loadings.astype(BF16)


def per_device(data, start, link_dev, link_slot, link_weight):
    devices = lax.axis_size("cells")
    groups = lax.axis_size("genes")
    tiles_here, neighbours = link_dev.shape
    cells_here, genes_here = data.shape
    tile_cells = cells_here // tiles_here
    genes_total = genes_here * groups
    width = start.shape[1]
    part = width // groups
    tiles_all = tiles_here * devices
    rings = devices // RING
    depth = RING // 2
    lanes = 512
    spare = lanes - genes_here
    half = lanes // 2
    table = jnp.concatenate([link_dev, link_slot, link_weight], axis=1).astype(BF16)
    table = table.reshape(tiles_here, 1, TURNS, spare)
    table = jnp.broadcast_to(table, (tiles_here, tile_cells // TURNS, TURNS, spare))
    packed = jnp.concatenate(
        [data.reshape(tiles_here, tile_cells, genes_here), table.reshape(tiles_here, tile_cells, spare)], axis=2
    )
    packed = packed.reshape(tiles_here, RING, tile_cells // RING, lanes)

    vmem = pl.BlockSpec(memory_space=pltpu.VMEM)
    dma = pltpu.SemaphoreType.DMA
    sems = []
    for count in (RING, rings, rings, RING, RING, rings):
        sems += [dma((count,)), dma((count,))]
    for count in (groups, groups, RING, rings, RING, groups):
        sems += [dma((ITERS, count)), dma((ITERS, count))]
    rows = TURNS * tiles_all
    return pl.pallas_call(
        lambda *refs: power_kernel(genes_total, genes_here, groups, rings, *refs),
        out_shape=(
            jax.ShapeDtypeStruct((genes_here, width), F32),
            jax.ShapeDtypeStruct((part, cells_here), BF16),
        ),
        in_specs=[vmem] * 2,
        out_specs=(vmem, vmem),
        scratch_shapes=[
            pltpu.VMEM((RING, tiles_here, 16, half), BF16),
            pltpu.VMEM((rings, depth // 2, 32, half), BF16),
            pltpu.VMEM((rings, depth // 2, 32, half), BF16),
            pltpu.VMEM((rings, tiles_here, 32, half), BF16),
            pltpu.VMEM((rings, tiles_here, 32, half), BF16),
            pltpu.VMEM((RING, depth // 2, 16, half), BF16),
            pltpu.VMEM((RING, depth // 2, 16, half), BF16),
            pltpu.VMEM((TURNS, tiles_all, lanes), BF16),
            pltpu.VMEM((tiles_all, tiles_all), BF16),
            pltpu.VMEM((tiles_all, tiles_all), BF16),
            pltpu.VMEM((rows, lanes), BF16),
            pltpu.VMEM((lanes, rows), BF16),
            pltpu.VMEM((RING, 32, 128), BF16),
            pltpu.VMEM((RING, 32, 128), BF16),
            pltpu.VMEM((rings, 64, 128), BF16),
            pltpu.VMEM((rings, 64, 128), BF16),
            pltpu.VMEM((ITERS, groups, part, rows), BF16),
            pltpu.VMEM((ITERS, groups, part, rows), BF16),
            pltpu.VMEM((ITERS, groups, part, rows), BF16),
            pltpu.VMEM((ITERS, RING, 8, half), F32),
            pltpu.VMEM((ITERS, RING, 8, half), F32),
            pltpu.VMEM((ITERS, rings, 8, half), F32),
            pltpu.VMEM((ITERS, RING, 8, half), F32),
            pltpu.VMEM((ITERS, groups, width, width), F32),
            pltpu.VMEM((width, lanes), F32),
            pltpu.VMEM((width, lanes), BF16),
            pltpu.VMEM((lanes, width), F32),
            *sems,
        ],
        compiler_params=pltpu.CompilerParams(collective_id=0, has_side_effects=True),
        name="power",
    )(packed, start)


def solution(mesh):
    placed = (
        P("cells", "genes"),
        P("genes", None),
        P("cells", None),
        P("cells", None),
        P("cells", None),
    )
    return jax.shard_map(
        per_device,
        mesh=mesh,
        in_specs=placed,
        out_specs=(P("genes", None), P("genes", "cells")),
        check_vma=False,
    )
```

```python
import math

import jax
import jax.numpy as jnp
from jax import lax
from jax.experimental import pallas as pl
from jax.experimental.pallas import tpu as pltpu
from jax.sharding import PartitionSpec as P

ITERS = 3
MESH = pl.DeviceIdType.MESH
SELF = 8.0
RING = 16
TILES, TURNS = 4, 2
F32, BF16 = jnp.float32, jnp.bfloat16
HIGH = lax.Precision.HIGHEST


def inverse_factor(gram):
    n = gram.shape[0]
    count = n // 8
    row_at = lax.broadcasted_iota(jnp.int32, (8, 2 * n), 0)
    lane_at = lax.broadcasted_iota(jnp.int32, (8, 2 * n), 1)
    wide = lambda v: jnp.broadcast_to(v, (8, 2 * n))
    parts = [jnp.where(lane_at == row_at + 8 * b, gram[8 * b : 8 * b + 8], 0.0) for b in range(count)]
    down = [wide(lax.rsqrt(jnp.sum(p, axis=1, keepdims=True))) for p in parts]
    total = parts[0]
    for p in parts[1:]:
        total = total + p
    across = jnp.where(lane_at < n, wide(jnp.sum(total, axis=0, keepdims=True)), 1.0)
    across = lax.rsqrt(across)
    blocks = []
    for b in range(count):
        right = jnp.where(lane_at == row_at + (n + 8 * b), down[b], 0.0)
        blocks.append(jnp.where(lane_at < n, gram[8 * b : 8 * b + 8] * down[b] * across, right))
    rows = []
    for k in range(0, n, 4):
        at, sub = divmod(k, 8)
        r = [wide(blocks[at][sub + i : sub + i + 1]) for i in range(4)]
        s = {(i, j): wide(r[i][:, k + j : k + j + 1]) for i in range(4) for j in range(i, 4)}
        here = range(at, count)
        c = {(b, i): wide(blocks[b][:, k + i : k + i + 1]) for b in here for i in range(4)}
        det = s[0, 0] * s[1, 1] - s[0, 1] * s[0, 1]
        inv = 1.0 / det
        solve = lambda u, v: ((u * s[1, 1] - v * s[0, 1]) * inv, (v * s[0, 0] - u * s[0, 1]) * inv)
        f2, f3 = solve(s[0, 2], s[1, 2]), solve(s[0, 3], s[1, 3])
        r2 = r[2] - f2[0] * r[0] - f2[1] * r[1]
        r3 = r[3] - f3[0] * r[0] - f3[1] * r[1]
        s22 = s[2, 2] - f2[0] * s[0, 2] - f2[1] * s[1, 2]
        s23 = s[2, 3] - f2[0] * s[0, 3] - f2[1] * s[1, 3]
        s33 = s[3, 3] - f3[0] * s[0, 3] - f3[1] * s[1, 3]
        det2 = s22 * s33 - s23 * s23
        inv2 = 1.0 / det2
        for b in here:
            if b == at and sub:
                continue
            l0, l1 = solve(c[b, 0], c[b, 1])
            c2 = c[b, 2] - l0 * s[0, 2] - l1 * s[1, 2]
            c3 = c[b, 3] - l0 * s[0, 3] - l1 * s[1, 3]
            l2 = (c2 * s33 - c3 * s23) * inv2
            l3 = (c3 * s22 - c2 * s23) * inv2
            change = l0 * r[0] + l1 * r[1] + l2 * r2 + l3 * r3
            if b == at:
                change = jnp.where(row_at >= 4, change, 0.0)
            blocks[b] = blocks[b] - change
        low, low2 = s[0, 1] / s[0, 0], s23 / s22
        rows.append(r[0] * lax.rsqrt(s[0, 0]))
        rows.append((r[1] - low * r[0]) * lax.rsqrt(s[1, 1] - low * s[0, 1]))
        rows.append(r2 * lax.rsqrt(s22))
        rows.append((r3 - low2 * r2) * lax.rsqrt(s33 - low2 * s23))
    out = []
    for b in range(count):
        block = rows[8 * b]
        for i in range(1, 8):
            block = jnp.where(row_at == i, rows[8 * b + i], block)
        out.append(block[:, n:])
    return jnp.concatenate(out, axis=0)


def one_hot(outs, ins, place):
    row = lax.broadcasted_iota(jnp.int32, (outs, ins), 0)
    column = lax.broadcasted_iota(jnp.int32, (outs, ins), 1)
    return (column == place(row)).astype(F32).astype(BF16)


def pick(matrix, rows):
    return jnp.dot(matrix, rows, preferred_element_type=F32).astype(BF16)


NT = (((1,), (1,)), ((), ()))


def power_kernel(
    genes_total, genes_here, groups, rings,
    data_ref, table_ref, start_ref,
    q_out, s_out,
    x_ref, xb_ref, a1_send, a1_got, a2_send, a2_got, b1_send, b1_got, b2_send, b2_got, d_ref, tab_ref, turn_ref, links_ref, tail_ref, y_ref, yt_ref,
    f1_send, f1_got, f2_send, f2_got,
    z_send, z_got, s_got, u_send, u_got, v_got, w_got, g_got, full, q_ref,
    in_sem,
    a1_ss, a1_rs, a2_ss, a2_rs, b1_ss, b1_rs, b2_ss, b2_rs, f1_ss, f1_rs, f2_ss, f2_rs,
    z_ss, z_rs, s_ss, s_rs, u_ss, u_rs, v_ss, v_rs, w_ss, w_rs, g_ss, g_rs,
):
    cell, group = lax.axis_index("cells"), lax.axis_index("genes")
    ring, spot = cell // RING, lax.rem(cell, RING)
    layer, core = spot // 2, lax.rem(spot, 2)
    depth = RING // 2
    far = lambda n: sorted(range(1, n), key=lambda d: (-min(d, n - d), d))
    x_peers = [((cell, lax.rem(group + d, groups)), lax.rem(group + d, groups)) for d in far(groups)]
    z_peers = []
    for d in far(depth) + [0]:
        for e in (0, 1):
            if d or e:
                at = lax.rem(layer + d, depth) * 2 + lax.rem(core + e, 2)
                z_peers.append(((ring * RING + at, group), at))
    y_peers = [
        ((lax.rem(ring + d, rings) * RING + spot, group), lax.rem(ring + d, rings)) for d in far(rings)
    ]
    barrier = pltpu.get_barrier_semaphore()
    for device, _ in x_peers + z_peers + y_peers:
        pl.semaphore_signal(barrier, inc=1, device_id=device, device_id_type=MESH)
    bring = pltpu.make_async_copy(data_ref, x_ref, in_sem)
    bring.start()

    def exchange(peers, me, source, got, send, receive):
        copies = [
            pltpu.make_async_remote_copy(
                src_ref=source(at), dst_ref=got.at[me], send_sem=send.at[at], recv_sem=receive.at[me],
                device_id=device, device_id_type=MESH,
            )
            for device, at in peers
        ]
        for copy in copies:
            copy.start()

        def finish():
            for device, at in peers:
                pltpu.make_async_remote_copy(
                    src_ref=source(at), dst_ref=got.at[at], send_sem=send.at[at], recv_sem=receive.at[at],
                    device_id=device, device_id_type=MESH,
                ).wait_recv()
            for copy in copies:
                copy.wait_send()

        return finish

    tiles, genes = d_ref.shape[1], d_ref.shape[2]
    width = start_ref.shape[0]
    part = width // groups
    half = genes // 2
    pairs = depth // 2

    order = one_hot(256, 256, lambda o: ((o >> 1) & 15) * 16 + (o >> 5) * 2 + (o & 1))
    plain = one_hot(256, 256, lambda o: o)
    turned = lambda matrix, cells: lax.dot_general(matrix, cells, NT, preferred_element_type=F32).astype(BF16)
    q_ref[...] = jnp.zeros(q_ref.shape, BF16)
    q_ref[:, 0:genes_here] = start_ref[...].astype(BF16)
    xb_ref[half - 16 :] = table_ref[...]
    bring.wait()
    for t in range(TILES):
        rows = turned(plain, x_ref[0:half, 256 * t : 256 * (t + 1)])
        a1_send[:, t] = rows.reshape(RING, 16, half)
    whole = genes_here // 16 * 16
    xb_ref[0 : whole - half] = x_ref[half:whole]
    xb_ref[whole - half : genes_here - half] = x_ref[whole:genes_here]
    pl.semaphore_wait(barrier, len(x_peers) + len(z_peers) + len(y_peers))
    finish_a1 = exchange(z_peers, spot, lambda at: a1_send.at[at], a1_got, a1_ss, a1_rs)
    for t in range(TILES):
        rows = turned(order, xb_ref[:, 256 * t : 256 * (t + 1)])
        b1_send[:, t] = rows.reshape(rings, 32, half)
    finish_b1 = exchange(y_peers, ring, lambda at: b1_send.at[at], b1_got, b1_ss, b1_rs)
    a1_got[spot] = a1_send[spot]
    b1_got[ring] = b1_send[ring]
    order_a = one_hot(256, 256, lambda o: ((o >> 3) & 3) * 64 + ((o >> 1) & 3) * 16 + (o >> 5) * 2 + (o & 1))
    order_b = one_hot(256, 256, lambda o: ((o >> 3) & 1) * 128 + ((o >> 1) & 3) * 32 + (o >> 4) * 2 + (o & 1))
    last_a = one_hot(256, 256, lambda o: (o & 127) * 2 + (o >> 7))
    last_b = one_hot(
        256, 256, lambda o: ((o >> 2) & 3) * 64 + ((o >> 4) & 7) * 8 + (o & 3) * 2 + (o >> 7)
    )
    finish_a1()
    for j in range(pairs):
        rows = pick(order_a, a1_got[4 * j : 4 * j + 4].reshape(256, half))
        a2_send[:, j] = rows.reshape(rings, 32, half)
    finish_a2 = exchange(y_peers, ring, lambda at: a2_send.at[at], a2_got, a2_ss, a2_rs)
    a2_got[ring] = a2_send[ring]
    finish_b1()
    for j in range(pairs):
        rows = pick(order_b, b1_got[2 * j : 2 * j + 2].reshape(256, half))
        b2_send[:, j] = rows.reshape(RING, 16, half)
    finish_b2 = exchange(z_peers, spot, lambda at: b2_send.at[at], b2_got, b2_ss, b2_rs)
    b2_got[spot] = b2_send[spot]
    finish_a2()
    for j in range(pairs):
        rows = pick(last_a, a2_got[2 * j : 2 * j + 2].reshape(256, half))
        for i in range(TURNS):
            d_ref[i, 128 * j : 128 * (j + 1), 0:half] = rows[128 * i : 128 * (i + 1)]
    finish_b2()
    for j in range(pairs):
        rows = pick(last_b, b2_got[4 * j : 4 * j + 4].reshape(256, half))
        for i in range(TURNS):
            for r in range(rings):
                d_ref[i, 64 * r + 16 * j : 64 * r + 16 * (j + 1), half:] = rows[
                    128 * i + 16 * r : 128 * i + 16 * (r + 1)
                ]

    root = math.sqrt(SELF / math.sqrt(genes_total))
    one = d_ref[0, :, genes - 128 :].astype(F32).T
    two = d_ref[1, :, genes - 128 :].astype(F32).T
    for j in range(8):
        place = one[124 + j : 125 + j] if j < 4 else two[112 + j : 113 + j]
        tab_ref[j : j + 1] = one[116 + j : 117 + j] * TILES + place
        tab_ref[8 + j : 9 + j] = two[120 + j : 121 + j]
    lane = lax.broadcasted_iota(jnp.int32, (32, tiles), 1)
    row_at = lax.broadcasted_iota(jnp.int32, (32, tiles), 0)

    def build(i, carry):
        at = pl.multiple_of(i * 32, 32)
        row = row_at + at
        links = jnp.where(lane == row, SELF, 0.0)
        row = row.astype(F32)
        for j in range(8):
            links = links + jnp.where(row == tab_ref[j : j + 1], tab_ref[8 + j : 9 + j], 0.0)
        turn_ref[pl.ds(at, 32)] = links.astype(BF16)
        return carry

    lax.fori_loop(0, tiles // 32, build, 0)
    links_ref[...] = turn_ref[...].T
    tail = d_ref[1, :, genes - 128 :].astype(F32)
    tail_lane = lax.broadcasted_iota(jnp.int32, tail.shape, 1)
    scale = root / (SELF + jnp.sum(jnp.where(tail_lane >= 120, tail, 0.0), axis=1, keepdims=True))
    gene_lane = lax.broadcasted_iota(jnp.int32, (tiles, genes), 1)
    for i in range(TURNS):
        rows = jnp.dot(links_ref[...], d_ref[i], preferred_element_type=F32) * scale
        rows = jnp.where(gene_lane < genes_here, rows, 0.0).astype(BF16)
        y_ref[tiles * i : tiles * (i + 1)] = rows
        yt_ref[:, tiles * i : tiles * (i + 1)] = rows.T

    for step in range(ITERS):
        final = step == ITERS - 1
        partial = jnp.dot(q_ref[...], yt_ref[...], preferred_element_type=F32).astype(BF16)
        for g in range(groups):
            z_send[step, g] = partial[part * g : part * (g + 1)]
        finish = exchange(x_peers, group, lambda at: z_send.at[step, at], z_got.at[step], z_ss.at[step], z_rs.at[step])
        z_got[step, group] = z_send[step, group]
        if final:
            tail_scale = root / (SELF + jnp.sum(tab_ref[8:16], axis=0, keepdims=True))
        finish()
        mine = z_got[step, 0].astype(F32)
        for g in range(1, groups):
            mine = mine + z_got[step, g].astype(F32)
        mine = mine.astype(BF16)
        s_got[step, group] = mine
        finish = exchange(x_peers, group, lambda at: s_got.at[step, group], s_got.at[step], s_ss.at[step], s_rs.at[step])
        if final:
            sent = [(mine[:, tiles * i : tiles * (i + 1)].astype(F32) * tail_scale).astype(BF16) for i in range(TURNS)]
            sent = jnp.concatenate(sent + [jnp.zeros((128 - TURNS * part, tiles), BF16)], axis=0)
            second = lax.dot_general(tail_ref[...], sent, NT, preferred_element_type=F32).astype(BF16)
            f1_send[...] = second.reshape(f1_send.shape)
            finish_f1 = exchange(z_peers, spot, lambda at: f1_send.at[at], f1_got, f1_ss, f1_rs)
            f1_got[spot] = f1_send[spot]
        finish()
        scores = jnp.concatenate([s_got[step, g] for g in range(groups)], axis=0)
        update = jnp.dot(scores, y_ref[...], preferred_element_type=F32)
        for s in range(RING):
            a, b = divmod(s, genes // 128)
            u_send[step, s] = update[16 * a : 16 * a + 16, 128 * b : 128 * b + 128].astype(BF16)
        finish = exchange(z_peers, spot, lambda at: u_send.at[step, at], u_got.at[step], u_ss.at[step], u_rs.at[step])
        u_got[step, spot] = u_send[step, spot]
        if step == 0:
            order = one_hot(tiles, tiles, lambda o: ((o >> 2) & 7) * 64 + (o >> 5) * 4 + (o & 3))
            tail_ref[...] = pick(order, turn_ref[...])
        if final:
            finish_f1()
            order = one_hot(tiles, tiles, lambda o: ((o >> 2) & 15) * 32 + (o >> 6) * 4 + (o & 3))
            f2_send[...] = pick(order, f1_got[...].reshape(tiles, 128)).reshape(f2_send.shape)
            finish_f2 = exchange(y_peers, ring, lambda at: f2_send.at[at], f2_got, f2_ss, f2_rs)
            f2_got[ring] = f2_send[ring]
        finish()
        total = u_got[step, 0].astype(F32)
        for s in range(1, RING):
            total = total + u_got[step, s].astype(F32)
        v_got[step, ring] = total
        finish = exchange(y_peers, ring, lambda at: v_got.at[step, ring], v_got.at[step], v_ss.at[step], v_rs.at[step])
        finish()
        total = v_got[step, 0]
        for s in range(1, rings):
            total = total + v_got[step, s]
        w_got[step, spot] = total
        finish = exchange(z_peers, spot, lambda at: w_got.at[step, spot], w_got.at[step], w_ss.at[step], w_rs.at[step])
        if final:
            finish_f2()
            turned = f2_got[...].reshape(tiles, 128).astype(F32).T.astype(BF16)
            cells = s_out.shape[1]
            row = lax.broadcasted_iota(jnp.int32, (tiles, cells), 0)
            column = lax.broadcasted_iota(jnp.int32, (tiles, cells), 1)
            spread = column == (row & 3) * 256 + ((row >> 2) & 15) * 16 + (row >> 6) * 2
            spread = spread.astype(F32).astype(BF16)
            even = jnp.dot(turned[0:part], spread, preferred_element_type=F32)
            odd = jnp.dot(turned[part : 2 * part], spread, preferred_element_type=F32)
            s_out[...] = (even + pltpu.roll(odd, 1, 1)).astype(BF16)
        finish()
        for s in range(RING):
            a, b = divmod(s, genes // 128)
            full[16 * a : 16 * a + 16, 128 * b : 128 * b + 128] = w_got[step, s]
        update = full[...]
        gram = lax.dot_general(update, update, NT, precision=HIGH, preferred_element_type=F32)
        g_got[step, group] = jnp.concatenate([gram[: width // 2], gram[width // 2 :]], axis=1)
        finish = exchange(x_peers, group, lambda at: g_got.at[step, group], g_got.at[step], g_ss.at[step], g_rs.at[step])
        finish()
        gram = g_got[step, 0]
        for g in range(1, groups):
            gram = gram + g_got[step, g]
        gram = gram * (1.0 / genes_total)
        gram = jnp.concatenate([gram, pltpu.roll(gram, width, 1)], axis=0)
        factor = inverse_factor(gram)
        loadings = jnp.dot(factor, full[...], precision=HIGH, preferred_element_type=F32)
        if final:
            q_out[...] = loadings[:, 0:genes_here]
        else:
            q_ref[...] = loadings.astype(BF16)


def per_device(data, start, link_dev, link_slot, link_weight):
    devices = lax.axis_size("cells")
    groups = lax.axis_size("genes")
    tiles_here, neighbours = link_dev.shape
    cells_here, genes_here = data.shape
    tile_cells = cells_here // tiles_here
    genes_total = genes_here * groups
    width = start.shape[1]
    part = width // groups
    tiles_all = tiles_here * devices
    rings = devices // RING
    depth = RING // 2
    lanes = 512
    spare = lanes - genes_here
    half = lanes // 2
    table = jnp.concatenate([link_dev, link_slot, link_weight], axis=1).astype(BF16)
    table = table.reshape(tiles_here * TURNS, spare).T.reshape(spare, tiles_here, 1, TURNS)
    table = jnp.broadcast_to(table, (spare, tiles_here, tile_cells // TURNS, TURNS)).reshape(spare, cells_here)
    table = jnp.pad(table, ((16 - spare, 0), (0, 0)))

    vmem = pl.BlockSpec(memory_space=pltpu.VMEM)
    dma = pltpu.SemaphoreType.DMA
    sems = []
    for count in (RING, rings, rings, RING, RING, rings):
        sems += [dma((count,)), dma((count,))]
    for count in (groups, groups, RING, rings, RING, groups):
        sems += [dma((ITERS, count)), dma((ITERS, count))]
    rows = TURNS * tiles_all
    loadings, smoothed = pl.pallas_call(
        lambda *refs: power_kernel(genes_total, genes_here, groups, rings, *refs),
        out_shape=(
            jax.ShapeDtypeStruct((width, genes_here), F32),
            jax.ShapeDtypeStruct((part, cells_here), BF16),
        ),
        in_specs=[pl.BlockSpec(memory_space=pl.ANY), vmem, vmem],
        out_specs=(vmem, vmem),
        scratch_shapes=[
            pltpu.VMEM((genes_here, cells_here), BF16),
            pltpu.VMEM((half, cells_here), BF16),
            pltpu.VMEM((RING, tiles_here, 16, half), BF16),
            pltpu.VMEM((RING, tiles_here, 16, half), BF16),
            pltpu.VMEM((rings, depth // 2, 32, half), BF16),
            pltpu.VMEM((rings, depth // 2, 32, half), BF16),
            pltpu.VMEM((rings, tiles_here, 32, half), BF16),
            pltpu.VMEM((rings, tiles_here, 32, half), BF16),
            pltpu.VMEM((RING, depth // 2, 16, half), BF16),
            pltpu.VMEM((RING, depth // 2, 16, half), BF16),
            pltpu.VMEM((TURNS, tiles_all, lanes), BF16),
            pltpu.VMEM((16, tiles_all), F32),
            pltpu.VMEM((tiles_all, tiles_all), BF16),
            pltpu.VMEM((tiles_all, tiles_all), BF16),
            pltpu.VMEM((tiles_all, tiles_all), BF16),
            pltpu.VMEM((rows, lanes), BF16),
            pltpu.VMEM((lanes, rows), BF16),
            pltpu.VMEM((RING, 32, 128), BF16),
            pltpu.VMEM((RING, 32, 128), BF16),
            pltpu.VMEM((rings, 64, 128), BF16),
            pltpu.VMEM((rings, 64, 128), BF16),
            pltpu.VMEM((ITERS, groups, part, rows), BF16),
            pltpu.VMEM((ITERS, groups, part, rows), BF16),
            pltpu.VMEM((ITERS, groups, part, rows), BF16),
            pltpu.VMEM((ITERS, RING, 16, 128), BF16),
            pltpu.VMEM((ITERS, RING, 16, 128), BF16),
            pltpu.VMEM((ITERS, rings, 16, 128), F32),
            pltpu.VMEM((ITERS, RING, 16, 128), F32),
            pltpu.VMEM((ITERS, groups, width // 2, 2 * width), F32),
            pltpu.VMEM((width, lanes), F32),
            pltpu.VMEM((width, lanes), BF16),
            dma,
            *sems,
        ],
        compiler_params=pltpu.CompilerParams(collective_id=0, has_side_effects=True),
        name="power",
    )(data.T, table, start.T)
    return loadings.T, smoothed


def solution(mesh):
    placed = (
        P("cells", "genes"),
        P("genes", None),
        P("cells", None),
        P("cells", None),
        P("cells", None),
    )
    return jax.shard_map(
        per_device,
        mesh=mesh,
        in_specs=placed,
        out_specs=(P("genes", None), P("genes", "cells")),
        check_vma=False,
    )
```

```python
import math

import jax
import jax.numpy as jnp
from jax import lax
from jax.experimental import pallas as pl
from jax.experimental.pallas import tpu as pltpu
from jax.sharding import PartitionSpec as P

ITERS = 3
MESH = pl.DeviceIdType.MESH
SELF = 8.0
RING = 16
TILES, TURNS = 4, 2
F32, BF16 = jnp.float32, jnp.bfloat16
HIGH = lax.Precision.HIGHEST


def inverse_factor(gram):
    n = gram.shape[0]
    count = n // 8
    row_at = lax.broadcasted_iota(jnp.int32, (8, 2 * n), 0)
    lane_at = lax.broadcasted_iota(jnp.int32, (8, 2 * n), 1)
    wide = lambda v: jnp.broadcast_to(v, (8, 2 * n))
    parts = [jnp.where(lane_at == row_at + 8 * b, gram[8 * b : 8 * b + 8], 0.0) for b in range(count)]
    down = [wide(lax.rsqrt(jnp.sum(p, axis=1, keepdims=True))) for p in parts]
    total = parts[0]
    for p in parts[1:]:
        total = total + p
    across = jnp.where(lane_at < n, wide(jnp.sum(total, axis=0, keepdims=True)), 1.0)
    across = lax.rsqrt(across)
    blocks = []
    for b in range(count):
        right = jnp.where(lane_at == row_at + (n + 8 * b), down[b], 0.0)
        blocks.append(jnp.where(lane_at < n, gram[8 * b : 8 * b + 8] * down[b] * across, right))
    rows = []
    for k in range(0, n, 4):
        at, sub = divmod(k, 8)
        r = [wide(blocks[at][sub + i : sub + i + 1]) for i in range(4)]
        s = {(i, j): wide(r[i][:, k + j : k + j + 1]) for i in range(4) for j in range(i, 4)}
        here = range(at, count)
        c = {(b, i): wide(blocks[b][:, k + i : k + i + 1]) for b in here for i in range(4)}
        det = s[0, 0] * s[1, 1] - s[0, 1] * s[0, 1]
        inv = 1.0 / det
        solve = lambda u, v: ((u * s[1, 1] - v * s[0, 1]) * inv, (v * s[0, 0] - u * s[0, 1]) * inv)
        f2, f3 = solve(s[0, 2], s[1, 2]), solve(s[0, 3], s[1, 3])
        r2 = r[2] - f2[0] * r[0] - f2[1] * r[1]
        r3 = r[3] - f3[0] * r[0] - f3[1] * r[1]
        s22 = s[2, 2] - f2[0] * s[0, 2] - f2[1] * s[1, 2]
        s23 = s[2, 3] - f2[0] * s[0, 3] - f2[1] * s[1, 3]
        s33 = s[3, 3] - f3[0] * s[0, 3] - f3[1] * s[1, 3]
        det2 = s22 * s33 - s23 * s23
        inv2 = 1.0 / det2
        for b in here:
            if b == at and sub:
                continue
            l0, l1 = solve(c[b, 0], c[b, 1])
            c2 = c[b, 2] - l0 * s[0, 2] - l1 * s[1, 2]
            c3 = c[b, 3] - l0 * s[0, 3] - l1 * s[1, 3]
            l2 = (c2 * s33 - c3 * s23) * inv2
            l3 = (c3 * s22 - c2 * s23) * inv2
            change = l0 * r[0] + l1 * r[1] + l2 * r2 + l3 * r3
            if b == at:
                change = jnp.where(row_at >= 4, change, 0.0)
            blocks[b] = blocks[b] - change
        low, low2 = s[0, 1] / s[0, 0], s23 / s22
        rows.append(r[0] * lax.rsqrt(s[0, 0]))
        rows.append((r[1] - low * r[0]) * lax.rsqrt(s[1, 1] - low * s[0, 1]))
        rows.append(r2 * lax.rsqrt(s22))
        rows.append((r3 - low2 * r2) * lax.rsqrt(s33 - low2 * s23))
    out = []
    for b in range(count):
        block = rows[8 * b]
        for i in range(1, 8):
            block = jnp.where(row_at == i, rows[8 * b + i], block)
        out.append(block[:, n:])
    return jnp.concatenate(out, axis=0)


def one_hot(outs, ins, place):
    row = lax.broadcasted_iota(jnp.int32, (outs, ins), 0)
    column = lax.broadcasted_iota(jnp.int32, (outs, ins), 1)
    return (column == place(row)).astype(F32).astype(BF16)


def pick(matrix, rows):
    return jnp.dot(matrix, rows, preferred_element_type=F32).astype(BF16)


NT = (((1,), (1,)), ((), ()))


def power_kernel(
    genes_total, genes_here, groups, rings,
    data_ref, start_ref, dev_ref, slot_ref, weight_ref,
    q_out, s_out,
    x_ref, q0_ref, t0_ref, t1_ref, t2_ref, xb_ref, a1_send, a1_got, a2_send, a2_got, b1_send, b1_got, b2_send, b2_got, d_ref, tab_ref, turn_ref, links_ref, tail_ref, y_ref, yt_ref,
    f1_send, f1_got, f2_send, f2_got,
    z_send, z_got, s_got, u_send, u_got, v_got, w_got, g_got, full, q_ref,
    in_sem,
    a1_ss, a1_rs, a2_ss, a2_rs, b1_ss, b1_rs, b2_ss, b2_rs, f1_ss, f1_rs, f2_ss, f2_rs,
    z_ss, z_rs, s_ss, s_rs, u_ss, u_rs, v_ss, v_rs, w_ss, w_rs, g_ss, g_rs,
):
    cell, group = lax.axis_index("cells"), lax.axis_index("genes")
    ring, spot = cell // RING, lax.rem(cell, RING)
    layer, core = spot // 2, lax.rem(spot, 2)
    depth = RING // 2
    far = lambda n: sorted(range(1, n), key=lambda d: (-min(d, n - d), d))
    x_peers = [((cell, lax.rem(group + d, groups)), lax.rem(group + d, groups)) for d in far(groups)]
    z_peers = []
    for d in far(depth) + [0]:
        for e in (0, 1):
            if d or e:
                at = lax.rem(layer + d, depth) * 2 + lax.rem(core + e, 2)
                z_peers.append(((ring * RING + at, group), at))
    y_peers = [
        ((lax.rem(ring + d, rings) * RING + spot, group), lax.rem(ring + d, rings)) for d in far(rings)
    ]
    barrier = pltpu.get_barrier_semaphore()
    for device, _ in x_peers + z_peers + y_peers:
        pl.semaphore_signal(barrier, inc=1, device_id=device, device_id_type=MESH)
    bring = [
        pltpu.make_async_copy(source, own, in_sem.at[i])
        for i, (source, own) in enumerate(
            [(dev_ref, t0_ref), (slot_ref, t1_ref), (weight_ref, t2_ref), (start_ref, q0_ref), (data_ref, x_ref)]
        )
    ]
    for copy in bring:
        copy.start()

    def exchange(peers, me, source, got, send, receive):
        copies = [
            pltpu.make_async_remote_copy(
                src_ref=source(at), dst_ref=got.at[me], send_sem=send.at[at], recv_sem=receive.at[me],
                device_id=device, device_id_type=MESH,
            )
            for device, at in peers
        ]
        for copy in copies:
            copy.start()

        def finish():
            for device, at in peers:
                pltpu.make_async_remote_copy(
                    src_ref=source(at), dst_ref=got.at[at], send_sem=send.at[at], recv_sem=receive.at[at],
                    device_id=device, device_id_type=MESH,
                ).wait_recv()
            for copy in copies:
                copy.wait_send()

        return finish

    tiles, genes = d_ref.shape[1], d_ref.shape[2]
    width = start_ref.shape[0]
    part = width // groups
    half = genes // 2
    pairs = depth // 2

    order = one_hot(256, 256, lambda o: ((o >> 1) & 15) * 16 + (o >> 5) * 2 + (o & 1))
    plain = one_hot(256, 256, lambda o: o)
    turned = lambda matrix, cells: lax.dot_general(matrix, cells, NT, preferred_element_type=F32).astype(BF16)
    chunks = a1_send.shape[0]
    strip = half // chunks
    cells = x_ref.shape[1]
    at_cell = lax.broadcasted_iota(jnp.int32, (TILES, cells), 1)
    at_tile = lax.broadcasted_iota(jnp.int32, (TILES, cells), 0)
    for copy in bring[:4]:
        copy.wait()
    q_ref[...] = jnp.zeros(q_ref.shape, BF16)
    q_ref[:, 0:genes_here] = q0_ref[...].astype(BF16)
    table = jnp.zeros((16, cells), F32)
    for parity, columns in ((0, ((t0_ref, 4), (t1_ref, 12))), (1, ((t1_ref, 0), (t2_ref, 8)))):
        values = jnp.zeros((16, TILES), F32)
        for ref, shift in columns:
            column = one_hot(16, ref.shape[1], lambda o: o - shift)
            entries = ref[...].astype(F32).astype(BF16)
            values = values + lax.dot_general(column, entries, NT, preferred_element_type=F32)
        where = (at_cell >> 8 == at_tile) & (at_cell & 1 == parity)
        table = table + jnp.dot(values.astype(BF16), where.astype(F32).astype(BF16), preferred_element_type=F32)
    xb_ref[half - 16 :] = table.astype(BF16)
    bring[4].wait()
    for c in range(chunks):
        for t in range(TILES):
            rows = turned(plain, x_ref[strip * c : strip * (c + 1), 256 * t : 256 * (t + 1)])
            a1_send[c, :, t] = rows.reshape(RING, 16, strip)
    whole = genes_here // 16 * 16
    xb_ref[0 : whole - half] = x_ref[half:whole]
    xb_ref[whole - half : genes_here - half] = x_ref[whole:genes_here]
    for c in range(chunks):
        for t in range(TILES):
            rows = turned(order, xb_ref[strip * c : strip * (c + 1), 256 * t : 256 * (t + 1)])
            b1_send[c, :, t] = rows.reshape(rings, 32, strip)
    pl.semaphore_wait(barrier, len(x_peers) + len(z_peers) + len(y_peers))

    def over_z(c, send, got, send_sem, receive):
        return exchange(z_peers, spot, lambda at: send.at[c, at], got.at[c], send_sem.at[c], receive.at[c])

    def over_y(c, send, got, send_sem, receive):
        return exchange(y_peers, ring, lambda at: send.at[c, at], got.at[c], send_sem.at[c], receive.at[c])

    finish_a1, finish_b1, finish_a2, finish_b2 = [], [], [], []
    for c in range(chunks):
        finish_a1.append(over_z(c, a1_send, a1_got, a1_ss, a1_rs))
        finish_b1.append(over_y(c, b1_send, b1_got, b1_ss, b1_rs))
    for c in range(chunks):
        a1_got[c, spot] = a1_send[c, spot]
        b1_got[c, ring] = b1_send[c, ring]
    order_a = one_hot(256, 256, lambda o: ((o >> 3) & 3) * 64 + ((o >> 1) & 3) * 16 + (o >> 5) * 2 + (o & 1))
    order_b = one_hot(256, 256, lambda o: ((o >> 3) & 1) * 128 + ((o >> 1) & 3) * 32 + (o >> 4) * 2 + (o & 1))
    last_a = one_hot(256, 256, lambda o: (o & 127) * 2 + (o >> 7))
    last_b = one_hot(
        256, 256, lambda o: ((o >> 2) & 3) * 64 + ((o >> 4) & 7) * 8 + (o & 3) * 2 + (o >> 7)
    )
    for c in range(chunks):
        finish_a1[c]()
        for j in range(pairs):
            rows = pick(order_a, a1_got[c, 4 * j : 4 * j + 4].reshape(256, strip))
            a2_send[c, :, j] = rows.reshape(rings, 32, strip)
        finish_a2.append(over_y(c, a2_send, a2_got, a2_ss, a2_rs))
        a2_got[c, ring] = a2_send[c, ring]
        finish_b1[c]()
        for j in range(pairs):
            rows = pick(order_b, b1_got[c, 2 * j : 2 * j + 2].reshape(256, strip))
            b2_send[c, :, j] = rows.reshape(RING, 16, strip)
        finish_b2.append(over_z(c, b2_send, b2_got, b2_ss, b2_rs))
        b2_got[c, spot] = b2_send[c, spot]
    for c in range(chunks):
        finish_a2[c]()
        lanes = slice(strip * c, strip * (c + 1))
        for j in range(pairs):
            rows = pick(last_a, a2_got[c, 2 * j : 2 * j + 2].reshape(256, strip))
            for i in range(TURNS):
                d_ref[i, 128 * j : 128 * (j + 1), lanes] = rows[128 * i : 128 * (i + 1)]
        finish_b2[c]()
        lanes = slice(half + strip * c, half + strip * (c + 1))
        for j in range(pairs):
            rows = pick(last_b, b2_got[c, 4 * j : 4 * j + 4].reshape(256, strip))
            for i in range(TURNS):
                for r in range(rings):
                    d_ref[i, 64 * r + 16 * j : 64 * r + 16 * (j + 1), lanes] = rows[
                        128 * i + 16 * r : 128 * i + 16 * (r + 1)
                    ]

    root = math.sqrt(SELF / math.sqrt(genes_total))
    one = d_ref[0, :, genes - 128 :].astype(F32).T
    two = d_ref[1, :, genes - 128 :].astype(F32).T
    for j in range(8):
        place = one[124 + j : 125 + j] if j < 4 else two[112 + j : 113 + j]
        tab_ref[j : j + 1] = one[116 + j : 117 + j] * TILES + place
        tab_ref[8 + j : 9 + j] = two[120 + j : 121 + j]
    lane = lax.broadcasted_iota(jnp.int32, (32, tiles), 1)
    row_at = lax.broadcasted_iota(jnp.int32, (32, tiles), 0)

    def build(i, carry):
        at = pl.multiple_of(i * 32, 32)
        row = row_at + at
        links = jnp.where(lane == row, SELF, 0.0)
        row = row.astype(F32)
        for j in range(8):
            links = links + jnp.where(row == tab_ref[j : j + 1], tab_ref[8 + j : 9 + j], 0.0)
        turn_ref[pl.ds(at, 32)] = links.astype(BF16)
        return carry

    lax.fori_loop(0, tiles // 32, build, 0)
    links_ref[...] = turn_ref[...].T
    tail = d_ref[1, :, genes - 128 :].astype(F32)
    tail_lane = lax.broadcasted_iota(jnp.int32, tail.shape, 1)
    scale = root / (SELF + jnp.sum(jnp.where(tail_lane >= 120, tail, 0.0), axis=1, keepdims=True))
    gene_lane = lax.broadcasted_iota(jnp.int32, (tiles, genes), 1)
    for i in range(TURNS):
        rows = jnp.dot(links_ref[...], d_ref[i], preferred_element_type=F32) * scale
        rows = jnp.where(gene_lane < genes_here, rows, 0.0).astype(BF16)
        y_ref[tiles * i : tiles * (i + 1)] = rows
        yt_ref[:, tiles * i : tiles * (i + 1)] = rows.T

    for step in range(ITERS):
        final = step == ITERS - 1
        partial = jnp.dot(q_ref[...], yt_ref[...], preferred_element_type=F32).astype(BF16)
        for g in range(groups):
            z_send[step, g] = partial[part * g : part * (g + 1)]
        finish = exchange(x_peers, group, lambda at: z_send.at[step, at], z_got.at[step], z_ss.at[step], z_rs.at[step])
        z_got[step, group] = z_send[step, group]
        if final:
            tail_scale = root / (SELF + jnp.sum(tab_ref[8:16], axis=0, keepdims=True))
        finish()
        mine = z_got[step, 0].astype(F32)
        for g in range(1, groups):
            mine = mine + z_got[step, g].astype(F32)
        mine = mine.astype(BF16)
        s_got[step, group] = mine
        finish = exchange(x_peers, group, lambda at: s_got.at[step, group], s_got.at[step], s_ss.at[step], s_rs.at[step])
        if final:
            sent = [(mine[:, tiles * i : tiles * (i + 1)].astype(F32) * tail_scale).astype(BF16) for i in range(TURNS)]
            sent = jnp.concatenate(sent + [jnp.zeros((128 - TURNS * part, tiles), BF16)], axis=0)
            second = lax.dot_general(tail_ref[...], sent, NT, preferred_element_type=F32).astype(BF16)
            f1_send[...] = second.reshape(f1_send.shape)
            finish_f1 = exchange(z_peers, spot, lambda at: f1_send.at[at], f1_got, f1_ss, f1_rs)
            f1_got[spot] = f1_send[spot]
        finish()
        scores = jnp.concatenate([s_got[step, g] for g in range(groups)], axis=0)
        update = jnp.dot(scores, y_ref[...], preferred_element_type=F32)
        for s in range(RING):
            a, b = divmod(s, genes // 128)
            u_send[step, s] = update[16 * a : 16 * a + 16, 128 * b : 128 * b + 128].astype(BF16)
        finish = exchange(z_peers, spot, lambda at: u_send.at[step, at], u_got.at[step], u_ss.at[step], u_rs.at[step])
        u_got[step, spot] = u_send[step, spot]
        if step == 0:
            order = one_hot(tiles, tiles, lambda o: ((o >> 2) & 7) * 64 + (o >> 5) * 4 + (o & 3))
            tail_ref[...] = pick(order, turn_ref[...])
        if final:
            finish_f1()
            order = one_hot(tiles, tiles, lambda o: ((o >> 2) & 15) * 32 + (o >> 6) * 4 + (o & 3))
            f2_send[...] = pick(order, f1_got[...].reshape(tiles, 128)).reshape(f2_send.shape)
            finish_f2 = exchange(y_peers, ring, lambda at: f2_send.at[at], f2_got, f2_ss, f2_rs)
            f2_got[ring] = f2_send[ring]
        finish()
        total = u_got[step, 0].astype(F32)
        for s in range(1, RING):
            total = total + u_got[step, s].astype(F32)
        v_got[step, ring] = total
        finish = exchange(y_peers, ring, lambda at: v_got.at[step, ring], v_got.at[step], v_ss.at[step], v_rs.at[step])
        finish()
        total = v_got[step, 0]
        for s in range(1, rings):
            total = total + v_got[step, s]
        w_got[step, spot] = total
        finish = exchange(z_peers, spot, lambda at: w_got.at[step, spot], w_got.at[step], w_ss.at[step], w_rs.at[step])
        if final:
            finish_f2()
            turned = f2_got[...].reshape(tiles, 128).astype(F32).T.astype(BF16)
            row = lax.broadcasted_iota(jnp.int32, (tiles, cells), 0)
            column = lax.broadcasted_iota(jnp.int32, (tiles, cells), 1)
            spread = column == (row & 3) * 256 + ((row >> 2) & 15) * 16 + (row >> 6) * 2
            spread = spread.astype(F32).astype(BF16)
            even = jnp.dot(turned[0:part], spread, preferred_element_type=F32)
            odd = jnp.dot(turned[part : 2 * part], spread, preferred_element_type=F32)
            s_out[...] = (even + pltpu.roll(odd, 1, 1)).astype(BF16)
        finish()
        for s in range(RING):
            a, b = divmod(s, genes // 128)
            full[16 * a : 16 * a + 16, 128 * b : 128 * b + 128] = w_got[step, s]
        update = full[...]
        gram = lax.dot_general(update, update, NT, precision=HIGH, preferred_element_type=F32)
        g_got[step, group] = jnp.concatenate([gram[: width // 2], gram[width // 2 :]], axis=1)
        finish = exchange(x_peers, group, lambda at: g_got.at[step, group], g_got.at[step], g_ss.at[step], g_rs.at[step])
        finish()
        gram = g_got[step, 0]
        for g in range(1, groups):
            gram = gram + g_got[step, g]
        gram = gram * (1.0 / genes_total)
        gram = jnp.concatenate([gram, pltpu.roll(gram, width, 1)], axis=0)
        factor = inverse_factor(gram)
        loadings = jnp.dot(factor, full[...], precision=HIGH, preferred_element_type=F32)
        if final:
            q_out[...] = loadings[:, 0:genes_here]
        else:
            q_ref[...] = loadings.astype(BF16)


def per_device(data, start, link_dev, link_slot, link_weight):
    devices = lax.axis_size("cells")
    groups = lax.axis_size("genes")
    tiles_here, neighbours = link_dev.shape
    cells_here, genes_here = data.shape
    genes_total = genes_here * groups
    width = start.shape[1]
    part = width // groups
    tiles_all = tiles_here * devices
    rings = devices // RING
    depth = RING // 2
    lanes = 512
    half = lanes // 2
    chunks = 2
    strip = half // chunks
    vmem = pl.BlockSpec(memory_space=pltpu.VMEM)
    dma = pltpu.SemaphoreType.DMA
    sems = []
    for count in (RING, rings, rings, RING):
        sems += [dma((chunks, count)), dma((chunks, count))]
    for count in (RING, rings):
        sems += [dma((count,)), dma((count,))]
    for count in (groups, groups, RING, rings, RING, groups):
        sems += [dma((ITERS, count)), dma((ITERS, count))]
    rows = TURNS * tiles_all
    loadings, smoothed = pl.pallas_call(
        lambda *refs: power_kernel(genes_total, genes_here, groups, rings, *refs),
        out_shape=(
            jax.ShapeDtypeStruct((width, genes_here), F32),
            jax.ShapeDtypeStruct((part, cells_here), BF16),
        ),
        in_specs=[pl.BlockSpec(memory_space=pl.ANY)] * 5,
        out_specs=(vmem, vmem),
        scratch_shapes=[
            pltpu.VMEM((genes_here, cells_here), BF16),
            pltpu.VMEM((width, genes_here), F32),
            pltpu.VMEM((tiles_here, neighbours), jnp.int32),
            pltpu.VMEM((tiles_here, neighbours), jnp.int32),
            pltpu.VMEM((tiles_here, neighbours), jnp.int32),
            pltpu.VMEM((half, cells_here), BF16),
            pltpu.VMEM((chunks, RING, tiles_here, 16, strip), BF16),
            pltpu.VMEM((chunks, RING, tiles_here, 16, strip), BF16),
            pltpu.VMEM((chunks, rings, depth // 2, 32, strip), BF16),
            pltpu.VMEM((chunks, rings, depth // 2, 32, strip), BF16),
            pltpu.VMEM((chunks, rings, tiles_here, 32, strip), BF16),
            pltpu.VMEM((chunks, rings, tiles_here, 32, strip), BF16),
            pltpu.VMEM((chunks, RING, depth // 2, 16, strip), BF16),
            pltpu.VMEM((chunks, RING, depth // 2, 16, strip), BF16),
            pltpu.VMEM((TURNS, tiles_all, lanes), BF16),
            pltpu.VMEM((16, tiles_all), F32),
            pltpu.VMEM((tiles_all, tiles_all), BF16),
            pltpu.VMEM((tiles_all, tiles_all), BF16),
            pltpu.VMEM((tiles_all, tiles_all), BF16),
            pltpu.VMEM((rows, lanes), BF16),
            pltpu.VMEM((lanes, rows), BF16),
            pltpu.VMEM((RING, 32, 128), BF16),
            pltpu.VMEM((RING, 32, 128), BF16),
            pltpu.VMEM((rings, 64, 128), BF16),
            pltpu.VMEM((rings, 64, 128), BF16),
            pltpu.VMEM((ITERS, groups, part, rows), BF16),
            pltpu.VMEM((ITERS, groups, part, rows), BF16),
            pltpu.VMEM((ITERS, groups, part, rows), BF16),
            pltpu.VMEM((ITERS, RING, 16, 128), BF16),
            pltpu.VMEM((ITERS, RING, 16, 128), BF16),
            pltpu.VMEM((ITERS, rings, 16, 128), F32),
            pltpu.VMEM((ITERS, RING, 16, 128), F32),
            pltpu.VMEM((ITERS, groups, width // 2, 2 * width), F32),
            pltpu.VMEM((width, lanes), F32),
            pltpu.VMEM((width, lanes), BF16),
            dma((5,)),
            *sems,
        ],
        compiler_params=pltpu.CompilerParams(collective_id=0, has_side_effects=True),
        name="power",
    )(data.T, start.T, link_dev, link_slot, link_weight)
    return loadings.T, smoothed


def solution(mesh):
    placed = (
        P("cells", "genes"),
        P("genes", None),
        P("cells", None),
        P("cells", None),
        P("cells", None),
    )
    return jax.shard_map(
        per_device,
        mesh=mesh,
        in_specs=placed,
        out_specs=(P("genes", None), P("genes", "cells")),
        check_vma=False,
    )
```

```python
import math

import jax
import jax.numpy as jnp
from jax import lax
from jax.experimental import pallas as pl
from jax.experimental.pallas import tpu as pltpu
from jax.sharding import PartitionSpec as P

ITERS = 3
MESH = pl.DeviceIdType.MESH
SELF = 8.0
RING = 16
TILES, TURNS = 4, 2
F32, BF16 = jnp.float32, jnp.bfloat16
HIGH = lax.Precision.HIGHEST


def inverse_factor(gram):
    n = gram.shape[0]
    count = n // 8
    row_at = lax.broadcasted_iota(jnp.int32, (8, 2 * n), 0)
    lane_at = lax.broadcasted_iota(jnp.int32, (8, 2 * n), 1)
    wide = lambda v: jnp.broadcast_to(v, (8, 2 * n))
    parts = [jnp.where(lane_at == row_at + 8 * b, gram[8 * b : 8 * b + 8], 0.0) for b in range(count)]
    down = [wide(lax.rsqrt(jnp.sum(p, axis=1, keepdims=True))) for p in parts]
    total = parts[0]
    for p in parts[1:]:
        total = total + p
    across = jnp.where(lane_at < n, wide(jnp.sum(total, axis=0, keepdims=True)), 1.0)
    across = lax.rsqrt(across)
    blocks = []
    for b in range(count):
        right = jnp.where(lane_at == row_at + (n + 8 * b), down[b], 0.0)
        blocks.append(jnp.where(lane_at < n, gram[8 * b : 8 * b + 8] * down[b] * across, right))
    rows = []
    for at in range(count):
        r = [wide(blocks[at][i : i + 1]) for i in range(8)]
        s = {(i, j): wide(r[i][:, 8 * at + j : 8 * at + j + 1]) for i in range(8) for j in range(i, 8)}
        below = range(at + 1, count)
        c = {(b, i): wide(blocks[b][:, 8 * at + i : 8 * at + i + 1]) for b in below for i in range(8)}
        for p in range(0, 8, 2):
            q = p + 1
            inv = 1.0 / (s[p, p] * s[q, q] - s[p, q] * s[p, q])
            solve = lambda u, v: ((u * s[q, q] - v * s[p, q]) * inv, (v * s[p, p] - u * s[p, q]) * inv)
            low = s[p, q] / s[p, p]
            rows.append(r[p] * lax.rsqrt(s[p, p]))
            rows.append((r[q] - low * r[p]) * lax.rsqrt(s[q, q] - low * s[p, q]))
            for i in range(q + 1, 8):
                f, h = solve(s[p, i], s[q, i])
                r[i] = r[i] - f * r[p] - h * r[q]
                for j in range(i, 8):
                    s[i, j] = s[i, j] - f * s[p, j] - h * s[q, j]
            for b in below:
                f, h = solve(c[b, p], c[b, q])
                for i in range(q + 1, 8):
                    c[b, i] = c[b, i] - f * s[p, i] - h * s[q, i]
                blocks[b] = blocks[b] - f * r[p] - h * r[q]
    out = []
    for b in range(count):
        block = rows[8 * b]
        for i in range(1, 8):
            block = jnp.where(row_at == i, rows[8 * b + i], block)
        out.append(block[:, n:])
    return jnp.concatenate(out, axis=0)


def one_hot(outs, ins, place):
    row = lax.broadcasted_iota(jnp.int32, (outs, ins), 0)
    column = lax.broadcasted_iota(jnp.int32, (outs, ins), 1)
    return (column == place(row)).astype(F32).astype(BF16)


def pick(matrix, rows):
    return jnp.dot(matrix, rows, preferred_element_type=F32).astype(BF16)


NT = (((1,), (1,)), ((), ()))


def power_kernel(
    genes_total, genes_here, groups, rings,
    data_ref, start_ref, dev_ref, slot_ref, weight_ref,
    q_out, s_out,
    x_ref, q0_ref, t0_ref, t1_ref, t2_ref, xb_ref, a1_send, a1_got, a2_send, a2_got, b1_send, b1_got, b2_send, b2_got, d_ref, tab_ref, turn_ref, links_ref, tail_ref, y_ref, yt_ref,
    f1_send, f1_got, f2_send, f2_got,
    z_send, z_got, s_got, u_send, u_got, v_got, w_got, g_got, full, q_ref,
    in_sem,
    a1_ss, a1_rs, a2_ss, a2_rs, b1_ss, b1_rs, b2_ss, b2_rs, f1_ss, f1_rs, f2_ss, f2_rs,
    z_ss, z_rs, s_ss, s_rs, u_ss, u_rs, v_ss, v_rs, w_ss, w_rs, g_ss, g_rs, o_ss, o_rs,
):
    cell, group = lax.axis_index("cells"), lax.axis_index("genes")
    ring, spot = cell // RING, lax.rem(cell, RING)
    layer, core = spot // 2, lax.rem(spot, 2)
    depth = RING // 2
    far = lambda n: sorted(range(1, n), key=lambda d: (-min(d, n - d), d))
    x_peers = [((cell, lax.rem(group + d, groups)), lax.rem(group + d, groups)) for d in far(groups)]
    z_peers = []
    for d in far(depth) + [0]:
        for e in (0, 1):
            if d or e:
                at = lax.rem(layer + d, depth) * 2 + lax.rem(core + e, 2)
                z_peers.append(((ring * RING + at, group), at))
    y_peers = [
        ((lax.rem(ring + d, rings) * RING + spot, group), lax.rem(ring + d, rings)) for d in far(rings)
    ]
    core_peers = [((ring * RING + layer * 2 + 1 - core, group), 1 - core)]
    layer_peers = [
        ((ring * RING + lax.rem(layer + d, depth) * 2 + core, group), lax.rem(layer + d, depth)) for d in far(depth)
    ]
    wide_peers = []
    for d in far(groups) + [0]:
        for e in (0, 1):
            if d or e:
                other, beside = lax.rem(group + d, groups), lax.rem(core + e, 2)
                wide_peers.append(((ring * RING + layer * 2 + beside, other), other * 2 + beside))
    barrier = pltpu.get_barrier_semaphore()
    greeted = wide_peers + z_peers[:-1] + y_peers
    for device, _ in greeted:
        pl.semaphore_signal(barrier, inc=1, device_id=device, device_id_type=MESH)
    bring = [
        pltpu.make_async_copy(source, own, in_sem.at[i])
        for i, (source, own) in enumerate(
            [(dev_ref, t0_ref), (slot_ref, t1_ref), (weight_ref, t2_ref), (start_ref, q0_ref), (data_ref, x_ref)]
        )
    ]
    for copy in bring:
        copy.start()

    sent_copies = []

    def flush():
        for copy in sent_copies:
            copy.wait_send()
        sent_copies.clear()

    def exchange(peers, me, source, got, send, receive):
        copies = [
            pltpu.make_async_remote_copy(
                src_ref=source(at), dst_ref=got.at[me], send_sem=send.at[at], recv_sem=receive.at[me],
                device_id=device, device_id_type=MESH,
            )
            for device, at in peers
        ]
        for copy in copies:
            copy.start()

        def finish():
            flush()
            for device, at in peers:
                pltpu.make_async_remote_copy(
                    src_ref=source(at), dst_ref=got.at[at], send_sem=send.at[at], recv_sem=receive.at[at],
                    device_id=device, device_id_type=MESH,
                ).wait_recv()
            sent_copies.extend(copies)

        return finish

    tiles, genes = d_ref.shape[1], d_ref.shape[2]
    width = start_ref.shape[0]
    part = width // groups
    half = genes // 2
    pairs = depth // 2

    order = one_hot(256, 256, lambda o: ((o >> 1) & 15) * 16 + (o >> 5) * 2 + (o & 1))
    plain = one_hot(256, 256, lambda o: o)
    turned = lambda matrix, cells: lax.dot_general(matrix, cells, NT, preferred_element_type=F32).astype(BF16)
    chunks = a1_send.shape[0]
    strip = half // chunks
    cells = x_ref.shape[1]
    at_cell = lax.broadcasted_iota(jnp.int32, (TILES, cells), 1)
    at_tile = lax.broadcasted_iota(jnp.int32, (TILES, cells), 0)
    for copy in bring[:4]:
        copy.wait()
    q_ref[...] = jnp.zeros(q_ref.shape, BF16)
    q_ref[:, 0:genes_here] = q0_ref[...].astype(BF16)
    table = jnp.zeros((16, cells), F32)
    for parity, columns in ((0, ((t0_ref, 4), (t1_ref, 12))), (1, ((t1_ref, 0), (t2_ref, 8)))):
        values = jnp.zeros((16, TILES), F32)
        for ref, shift in columns:
            column = one_hot(16, ref.shape[1], lambda o: o - shift)
            entries = ref[...].astype(F32).astype(BF16)
            values = values + lax.dot_general(column, entries, NT, preferred_element_type=F32)
        where = (at_cell >> 8 == at_tile) & (at_cell & 1 == parity)
        table = table + jnp.dot(values.astype(BF16), where.astype(F32).astype(BF16), preferred_element_type=F32)
    xb_ref[half - 16 :] = table.astype(BF16)
    bring[4].wait()
    for c in range(chunks):
        for t in range(TILES):
            rows = turned(plain, x_ref[strip * c : strip * (c + 1), 256 * t : 256 * (t + 1)])
            a1_send[c, :, t] = rows.reshape(RING, 16, strip)
    whole = genes_here // 16 * 16
    xb_ref[0 : whole - half] = x_ref[half:whole]
    xb_ref[whole - half : genes_here - half] = x_ref[whole:genes_here]
    for c in range(chunks):
        for t in range(TILES):
            rows = turned(order, xb_ref[strip * c : strip * (c + 1), 256 * t : 256 * (t + 1)])
            b1_send[c, :, t] = rows.reshape(rings, 32, strip)
    pl.semaphore_wait(barrier, len(greeted))

    def over_z(c, send, got, send_sem, receive):
        return exchange(z_peers, spot, lambda at: send.at[c, at], got.at[c], send_sem.at[c], receive.at[c])

    def over_y(c, send, got, send_sem, receive):
        return exchange(y_peers, ring, lambda at: send.at[c, at], got.at[c], send_sem.at[c], receive.at[c])

    finish_a1, finish_b1, finish_a2, finish_b2 = [], [], [], []
    turn = list(range(chunks))[::-1]
    for c in turn:
        finish_a1.append(over_z(c, a1_send, a1_got, a1_ss, a1_rs))
        finish_b1.append(over_y(c, b1_send, b1_got, b1_ss, b1_rs))
    for c in range(chunks):
        a1_got[c, spot] = a1_send[c, spot]
        b1_got[c, ring] = b1_send[c, ring]
    order_a = one_hot(256, 256, lambda o: ((o >> 3) & 3) * 64 + ((o >> 1) & 3) * 16 + (o >> 5) * 2 + (o & 1))
    order_b = one_hot(256, 256, lambda o: ((o >> 3) & 1) * 128 + ((o >> 1) & 3) * 32 + (o >> 4) * 2 + (o & 1))
    last_a = one_hot(256, 256, lambda o: (o & 127) * 2 + (o >> 7))
    last_b = one_hot(
        256, 256, lambda o: ((o >> 2) & 3) * 64 + ((o >> 4) & 7) * 8 + (o & 3) * 2 + (o >> 7)
    )
    for at, c in enumerate(turn):
        finish_a1[at]()
        for j in range(pairs):
            rows = pick(order_a, a1_got[c, 4 * j : 4 * j + 4].reshape(256, strip))
            a2_send[c, :, j] = rows.reshape(rings, 32, strip)
        finish_a2.append(over_y(c, a2_send, a2_got, a2_ss, a2_rs))
        a2_got[c, ring] = a2_send[c, ring]
        finish_b1[at]()
        for j in range(pairs):
            rows = pick(order_b, b1_got[c, 2 * j : 2 * j + 2].reshape(256, strip))
            b2_send[c, :, j] = rows.reshape(RING, 16, strip)
        finish_b2.append(over_z(c, b2_send, b2_got, b2_ss, b2_rs))
        b2_got[c, spot] = b2_send[c, spot]
    for at, c in enumerate(turn):
        finish_a2[at]()
        lanes = slice(strip * c, strip * (c + 1))
        for j in range(pairs):
            rows = pick(last_a, a2_got[c, 2 * j : 2 * j + 2].reshape(256, strip))
            for i in range(TURNS):
                d_ref[i, 128 * j : 128 * (j + 1), lanes] = rows[128 * i : 128 * (i + 1)]
        finish_b2[at]()
        lanes = slice(half + strip * c, half + strip * (c + 1))
        for j in range(pairs):
            rows = pick(last_b, b2_got[c, 4 * j : 4 * j + 4].reshape(256, strip))
            for i in range(TURNS):
                for r in range(rings):
                    d_ref[i, 64 * r + 16 * j : 64 * r + 16 * (j + 1), lanes] = rows[
                        128 * i + 16 * r : 128 * i + 16 * (r + 1)
                    ]
        if at == 0:
            root = math.sqrt(SELF / math.sqrt(genes_total))
            one = d_ref[0, :, genes - 128 :].astype(F32).T
            two = d_ref[1, :, genes - 128 :].astype(F32).T
            for j in range(8):
                place = one[124 + j : 125 + j] if j < 4 else two[112 + j : 113 + j]
                tab_ref[j : j + 1] = one[116 + j : 117 + j] * TILES + place
                tab_ref[8 + j : 9 + j] = two[120 + j : 121 + j]
            lane = lax.broadcasted_iota(jnp.int32, (32, tiles), 1)
            row_at = lax.broadcasted_iota(jnp.int32, (32, tiles), 0)

            def build(i, carry):
                at = pl.multiple_of(i * 32, 32)
                row = row_at + at
                links = jnp.where(lane == row, SELF, 0.0)
                row = row.astype(F32)
                for j in range(8):
                    links = links + jnp.where(row == tab_ref[j : j + 1], tab_ref[8 + j : 9 + j], 0.0)
                turn_ref[pl.ds(at, 32)] = links.astype(BF16)
                return carry

            lax.fori_loop(0, tiles // 32, build, 0)
            links_ref[...] = turn_ref[...].T
            tail = d_ref[1, :, genes - 128 :].astype(F32)
            tail_lane = lax.broadcasted_iota(jnp.int32, tail.shape, 1)
            scale = root / (SELF + jnp.sum(jnp.where(tail_lane >= 120, tail, 0.0), axis=1, keepdims=True))
    gene_lane = lax.broadcasted_iota(jnp.int32, (tiles, genes), 1)
    for i in range(TURNS):
        rows = jnp.dot(links_ref[...], d_ref[i], preferred_element_type=F32) * scale
        rows = jnp.where(gene_lane < genes_here, rows, 0.0).astype(BF16)
        y_ref[tiles * i : tiles * (i + 1)] = rows
        yt_ref[:, tiles * i : tiles * (i + 1)] = rows.T

    for step in range(ITERS):
        final = step == ITERS - 1
        finish = []
        for i in range(TURNS):
            columns = slice(tiles * i, tiles * (i + 1))
            partial = jnp.dot(q_ref[...], yt_ref[:, columns], preferred_element_type=F32).astype(BF16)
            z_send[step, i] = partial.reshape(groups, part, tiles)
            finish.append(
                exchange(x_peers, group, lambda at, i=i: z_send.at[step, i, at], z_got.at[step, i], z_ss.at[step, i], z_rs.at[step, i])
            )
            z_got[step, i, group] = z_send[step, i, group]
        if final:
            tail_scale = root / (SELF + jnp.sum(tab_ref[8:16], axis=0, keepdims=True))
        mine, finish_s = [], []
        for i in range(TURNS):
            finish[i]()
            total = z_got[step, i, 0].astype(F32)
            for g in range(1, groups):
                total = total + z_got[step, i, g].astype(F32)
            mine.append(total.astype(BF16))
            s_got[step, i, group] = mine[i]
            finish_s.append(
                exchange(x_peers, group, lambda at, i=i: s_got.at[step, i, group], s_got.at[step, i], s_ss.at[step, i], s_rs.at[step, i])
            )
        if final:
            sent = [(m.astype(F32) * tail_scale).astype(BF16) for m in mine]
            sent = jnp.concatenate(sent + [jnp.zeros((128 - TURNS * part, tiles), BF16)], axis=0)
            second = lax.dot_general(tail_ref[...], sent, NT, preferred_element_type=F32).astype(BF16)
            f1_send[...] = second.reshape(f1_send.shape)
            finish_f1 = exchange(z_peers, spot, lambda at: f1_send.at[at], f1_got, f1_ss, f1_rs)
            f1_got[spot] = f1_send[spot]
        update = None
        for i in range(TURNS):
            finish_s[i]()
            term = jnp.dot(
                s_got[step, i].reshape(width, tiles), y_ref[tiles * i : tiles * (i + 1)], preferred_element_type=F32
            )
            update = term if update is None else update + term
        for s in range(RING):
            a, b = s // 4, s % 2 * 2 + s // 2 % 2
            u_send[step, s] = update[16 * a : 16 * a + 16, 128 * b : 128 * b + 128].astype(BF16)
        finish = exchange(z_peers, spot, lambda at: u_send.at[step, at], u_got.at[step], u_ss.at[step], u_rs.at[step])
        u_got[step, spot] = u_send[step, spot]
        if step == 0:
            order = one_hot(tiles, tiles, lambda o: ((o >> 2) & 7) * 64 + (o >> 5) * 4 + (o & 3))
            tail_ref[...] = pick(order, turn_ref[...])
        if final:
            finish_f1()
            order = one_hot(tiles, tiles, lambda o: ((o >> 2) & 15) * 32 + (o >> 6) * 4 + (o & 3))
            f2_send[...] = pick(order, f1_got[...].reshape(tiles, 128)).reshape(f2_send.shape)
            finish_f2 = exchange(y_peers, ring, lambda at: f2_send.at[at], f2_got, f2_ss, f2_rs)
            f2_got[ring] = f2_send[ring]
        finish()
        total = u_got[step, 0].astype(F32)
        for s in range(1, RING):
            total = total + u_got[step, s].astype(F32)
        v_got[step, ring] = total
        finish = exchange(y_peers, ring, lambda at: v_got.at[step, ring], v_got.at[step], v_ss.at[step], v_rs.at[step])
        finish()
        total = v_got[step, 0]
        for s in range(1, rings):
            total = total + v_got[step, s]
        w_got[step, layer] = total
        finish = exchange(layer_peers, layer, lambda at: w_got.at[step, layer], w_got.at[step], w_ss.at[step], w_rs.at[step])
        if final:
            finish_f2()
            turned = f2_got[...].reshape(tiles, 128).astype(F32).T.astype(BF16)
            row = lax.broadcasted_iota(jnp.int32, (tiles, cells), 0)
            column = lax.broadcasted_iota(jnp.int32, (tiles, cells), 1)
            spread = column == (row & 3) * 256 + ((row >> 2) & 15) * 16 + (row >> 6) * 2
            spread = spread.astype(F32).astype(BF16)
            even = jnp.dot(turned[0:part], spread, preferred_element_type=F32)
            odd = jnp.dot(turned[part : 2 * part], spread, preferred_element_type=F32)
            s_out[...] = (even + pltpu.roll(odd, 1, 1)).astype(BF16)
        finish()
        for s in range(depth):
            a, b = divmod(s, 2)
            full[step, core, 16 * a : 16 * a + 16, 128 * b : 128 * b + 128] = w_got[step, s]
        update = full[step, core]
        gram = lax.dot_general(update, update, NT, precision=HIGH, preferred_element_type=F32)
        corner = group * 2 + core
        g_got[step, corner] = jnp.concatenate([gram[: width // 2], gram[width // 2 :]], axis=1)
        finish = exchange(wide_peers, corner, lambda at: g_got.at[step, corner], g_got.at[step], g_ss.at[step], g_rs.at[step])
        finish_o = exchange(core_peers, core, lambda at: full.at[step, core], full.at[step], o_ss.at[step], o_rs.at[step])
        finish()
        gram = g_got[step, 0]
        for g in range(1, 2 * groups):
            gram = gram + g_got[step, g]
        gram = gram * (1.0 / genes_total)
        gram = jnp.concatenate([gram, pltpu.roll(gram, width, 1)], axis=0)
        factor = inverse_factor(gram)
        finish_o()
        loadings = jnp.concatenate(
            [jnp.dot(factor, full[step, e], precision=HIGH, preferred_element_type=F32) for e in (0, 1)], axis=1
        )
        if final:
            q_out[...] = loadings[:, 0:genes_here]
            flush()
        else:
            q_ref[...] = loadings.astype(BF16)


def per_device(data, start, link_dev, link_slot, link_weight):
    devices = lax.axis_size("cells")
    groups = lax.axis_size("genes")
    tiles_here, neighbours = link_dev.shape
    cells_here, genes_here = data.shape
    genes_total = genes_here * groups
    width = start.shape[1]
    part = width // groups
    tiles_all = tiles_here * devices
    rings = devices // RING
    depth = RING // 2
    lanes = 512
    half = lanes // 2
    chunks = 2
    strip = half // chunks
    vmem = pl.BlockSpec(memory_space=pltpu.VMEM)
    dma = pltpu.SemaphoreType.DMA
    sems = []
    for count in (RING, rings, rings, RING):
        sems += [dma((chunks, count)), dma((chunks, count))]
    for count in (RING, rings):
        sems += [dma((count,)), dma((count,))]
    for count in (groups, groups):
        sems += [dma((ITERS, TURNS, count)), dma((ITERS, TURNS, count))]
    for count in (RING, rings, depth, 2 * groups, 2):
        sems += [dma((ITERS, count)), dma((ITERS, count))]
    rows = TURNS * tiles_all
    loadings, smoothed = pl.pallas_call(
        lambda *refs: power_kernel(genes_total, genes_here, groups, rings, *refs),
        out_shape=(
            jax.ShapeDtypeStruct((width, genes_here), F32),
            jax.ShapeDtypeStruct((part, cells_here), BF16),
        ),
        in_specs=[pl.BlockSpec(memory_space=pl.ANY)] * 5,
        out_specs=(vmem, vmem),
        scratch_shapes=[
            pltpu.VMEM((genes_here, cells_here), BF16),
            pltpu.VMEM((width, genes_here), F32),
            pltpu.VMEM((tiles_here, neighbours), jnp.int32),
            pltpu.VMEM((tiles_here, neighbours), jnp.int32),
            pltpu.VMEM((tiles_here, neighbours), jnp.int32),
            pltpu.VMEM((half, cells_here), BF16),
            pltpu.VMEM((chunks, RING, tiles_here, 16, strip), BF16),
            pltpu.VMEM((chunks, RING, tiles_here, 16, strip), BF16),
            pltpu.VMEM((chunks, rings, depth // 2, 32, strip), BF16),
            pltpu.VMEM((chunks, rings, depth // 2, 32, strip), BF16),
            pltpu.VMEM((chunks, rings, tiles_here, 32, strip), BF16),
            pltpu.VMEM((chunks, rings, tiles_here, 32, strip), BF16),
            pltpu.VMEM((chunks, RING, depth // 2, 16, strip), BF16),
            pltpu.VMEM((chunks, RING, depth // 2, 16, strip), BF16),
            pltpu.VMEM((TURNS, tiles_all, lanes), BF16),
            pltpu.VMEM((16, tiles_all), F32),
            pltpu.VMEM((tiles_all, tiles_all), BF16),
            pltpu.VMEM((tiles_all, tiles_all), BF16),
            pltpu.VMEM((tiles_all, tiles_all), BF16),
            pltpu.VMEM((rows, lanes), BF16),
            pltpu.VMEM((lanes, rows), BF16),
            pltpu.VMEM((RING, 32, 128), BF16),
            pltpu.VMEM((RING, 32, 128), BF16),
            pltpu.VMEM((rings, 64, 128), BF16),
            pltpu.VMEM((rings, 64, 128), BF16),
            pltpu.VMEM((ITERS, TURNS, groups, part, tiles_all), BF16),
            pltpu.VMEM((ITERS, TURNS, groups, part, tiles_all), BF16),
            pltpu.VMEM((ITERS, TURNS, groups, part, tiles_all), BF16),
            pltpu.VMEM((ITERS, RING, 16, 128), BF16),
            pltpu.VMEM((ITERS, RING, 16, 128), BF16),
            pltpu.VMEM((ITERS, rings, 16, 128), F32),
            pltpu.VMEM((ITERS, depth, 16, 128), F32),
            pltpu.VMEM((ITERS, 2 * groups, width // 2, 2 * width), F32),
            pltpu.VMEM((ITERS, 2, width, half), F32),
            pltpu.VMEM((width, lanes), BF16),
            dma((5,)),
            *sems,
        ],
        compiler_params=pltpu.CompilerParams(collective_id=0, has_side_effects=True),
        name="power",
    )(data.T, start.T, link_dev, link_slot, link_weight)
    return loadings.T, smoothed


def solution(mesh):
    placed = (
        P("cells", "genes"),
        P("genes", None),
        P("cells", None),
        P("cells", None),
        P("cells", None),
    )
    return jax.shard_map(
        per_device,
        mesh=mesh,
        in_specs=placed,
        out_specs=(P("genes", None), P("genes", "cells")),
        check_vma=False,
    )
```
